32 devices in a mesh: dp: 8 (over z, y), mp: 4 (over x, core).
Axes of the slice: x: 2, y: 2, z: 4, core: 2. Of those that a mesh axis runs over, the one named last changes fastest.
Arguments:
- query: bfloat16 [4096, 4096], P('dp', 'mp'), may hold values from -6 to 6
- passage: bfloat16 [4096, 4096], P('dp', 'mp'), may hold values from -6 to 6
- query_scale: bfloat16 [4096], P('dp'), may hold values from 0.4 to 2.5
- passage_scale: bfloat16 [4096], P('dp'), may hold values from 0.4 to 2.5
- partners: int32 [8, 3], P('dp'), may hold values from 0 to 3, as said below
- counts: int32 [8], replicated, may hold values from 256 to 512, as said below
Outputs:
- loss: float32 [], replicated
- grad_query: bfloat16 [4096, 4096], P('dp', 'mp')
- grad_passage: bfloat16 [4096, 4096], P('dp', 'mp')
The draws below stay inside these ranges and needn't reach their ends.
Inputs may be any that keep to these rules, and one draw needn't show every extreme that they name: `partners`: each nonzero entry of a row is a distinct distance; block 0 and the last 3 blocks use all 3 slots. `counts`: some block has all 512 rows valid.
All inputs are finite; a program needn't handle non-finite values.
Results may differ from the reference program's by a relative error of at most 0.004.
Values may be sent and summed in bfloat16 or wider, within the bound.
A program may use at most 64 MiB of HBM per device.

```python
import math
import jax
import jax.numpy as jnp
from jax import lax

D = 4096
BLOCK = 512
WIN = 3
PMAX = 3
BLOCKS = 8
ROWS = 4096


def embed_all(key):
    key_q = jax.random.fold_in(key, 101)
    key_p = jax.random.fold_in(key, 102)
    key_a = jax.random.fold_in(key, 104)
    key_b = jax.random.fold_in(key, 105)
    values_q = jnp.clip(jax.random.normal(key_q, (ROWS, D), jnp.float32), -6.0, 6.0)
    values_p = jnp.clip(jax.random.normal(key_p, (ROWS, D), jnp.float32), -6.0, 6.0)
    scale_q = jnp.exp(jax.random.uniform(key_a, (ROWS,), jnp.float32, math.log(0.5), math.log(2.0)))
    scale_p = jnp.exp(jax.random.uniform(key_b, (ROWS,), jnp.float32, math.log(0.5), math.log(2.0)))
    return (values_q, values_p, scale_q, scale_p)


def draw_query(key, part):
    return embed_all(key)[0].astype(jnp.bfloat16)


def draw_passage(key, part):
    return embed_all(key)[1].astype(jnp.bfloat16)


def draw_query_scale(key, part):
    return embed_all(key)[2].astype(jnp.bfloat16)


def draw_passage_scale(key, part):
    return embed_all(key)[3].astype(jnp.bfloat16)


def draw_partners(key, part):
    key_c = jax.random.fold_in(key, 201)
    key_o = jax.random.fold_in(key, 202)
    used = jax.random.randint(key_c, (BLOCKS,), 0, PMAX + 1)
    block_ids = jnp.arange(BLOCKS)
    forced = (block_ids == 0) | (block_ids >= BLOCKS - WIN)
    used = jnp.where(forced, PMAX, used)
    ranks = jax.random.randint(key_o, (BLOCKS, WIN), 0, 1 << 20) * WIN + jnp.arange(WIN)[None, :]
    order = jnp.argsort(ranks, axis=1)[:, :PMAX] + 1
    slot = jnp.arange(PMAX)[None, :]
    return jnp.where(slot < used[:, None], order, 0).astype(jnp.int32)


def draw_counts(key, part):
    key_c = jax.random.fold_in(key, 301)
    key_f = jax.random.fold_in(key, 302)
    values = jax.random.randint(key_c, (BLOCKS,), BLOCK // 2, BLOCK + 1)
    full = jax.random.randint(key_f, (), 0, BLOCKS)
    return jnp.where(jnp.arange(BLOCKS) == full, BLOCK, values).astype(jnp.int32)


def setup_inputs(seed: int = 0) -> dict:
    keys = jax.random.split(jax.random.key(seed), 7)
    query = draw_query(jax.random.fold_in(keys[6], 71), 0)
    passage = draw_passage(jax.random.fold_in(keys[6], 71), 0)
    query_scale = draw_query_scale(jax.random.fold_in(keys[6], 71), 0)
    passage_scale = draw_passage_scale(jax.random.fold_in(keys[6], 71), 0)
    partners = draw_partners(jax.random.fold_in(keys[6], 71), 0)
    counts = draw_counts(jax.random.fold_in(keys[6], 71), 0)
    return dict(query=query, passage=passage, query_scale=query_scale, passage_scale=passage_scale, partners=partners, counts=counts)


def reference(query, passage, query_scale, passage_scale, partners, counts):
    inv = 1.0 / math.sqrt(D)
    q3 = query.reshape(BLOCKS, BLOCK, D)
    p3 = passage.reshape(BLOCKS, BLOCK, D)
    qs3 = query_scale.astype(jnp.float32).reshape(BLOCKS, BLOCK)
    ps3 = passage_scale.astype(jnp.float32).reshape(BLOCKS, BLOCK)
    column = jnp.arange(BLOCK, dtype=jnp.int32)

    def make_tile(a, b):
        raw = jnp.dot(q3[a], p3[b].T, preferred_element_type=jnp.float32)
        return raw * (qs3[a] * inv)[:, None] * ps3[b][None, :]

    def forward(a):
        offs = partners[a]
        blocks = jnp.concatenate([a[None], (a + offs) % BLOCKS]).astype(jnp.int32)
        live = jnp.concatenate([jnp.array([True]), offs > 0])
        scores = jnp.stack([make_tile(a, blocks[k]) for k in range(1 + PMAX)])
        col_ok = live[:, None] & (column[None, :] < counts[blocks][:, None])
        masked = jnp.where(col_ok[:, None, :], scores, -jnp.inf)
        top = lax.optimization_barrier(jnp.max(masked, axis=(0, 2)))
        weights = jnp.exp(masked - top[None, :, None])
        total = lax.optimization_barrier(jnp.sum(weights, axis=(0, 2)))
        lse = top + jnp.log(total)
        valid = column < counts[a]
        positive = jnp.diagonal(scores[0])
        loss_sum = jnp.sum(jnp.where(valid, lse - positive, 0.0))
        grads = weights / total[None, :, None]
        target = (column[:, None] == column[None, :]).astype(jnp.float32)
        grads = jnp.concatenate([(grads[0] - target)[None], grads[1:]])
        grads = jnp.where(valid[None, :, None], grads, 0.0)
        key_weight = (grads * ps3[blocks][:, None, :]).astype(jnp.bfloat16)
        gq = jnp.zeros((BLOCK, D), jnp.float32)
        for k in range(1 + PMAX):
            gq = gq + jnp.dot(key_weight[k], p3[blocks[k]], preferred_element_type=jnp.float32)
        return (lse, loss_sum, gq.astype(jnp.bfloat16))
    lses, losses, gqs = lax.map(forward, jnp.arange(BLOCKS, dtype=jnp.int32))

    def backward(b):
        col_ok = column < counts[b]
        scores = make_tile(b, b)
        masked = jnp.where(col_ok[None, :], scores, -jnp.inf)
        grads = jnp.exp(masked - lses[b][:, None])
        grads = grads - (column[:, None] == column[None, :]).astype(jnp.float32)
        grads = jnp.where((column < counts[b])[:, None] & col_ok[None, :], grads, 0.0)
        row_weight = (grads * qs3[b][:, None]).astype(jnp.bfloat16)
        total = jnp.dot(row_weight.T, q3[b], preferred_element_type=jnp.float32)
        for offset in range(1, WIN + 1):
            a = ((b - offset) % BLOCKS).astype(jnp.int32)
            live = jnp.any(partners[a] == offset)
            scores = make_tile(a, b)
            masked = jnp.where(col_ok[None, :] & live, scores, -jnp.inf)
            grads = jnp.exp(masked - lses[a][:, None])
            grads = jnp.where((column < counts[a])[:, None], grads, 0.0)
            row_weight = (grads * qs3[a][:, None]).astype(jnp.bfloat16)
            part = jnp.dot(row_weight.T, q3[a], preferred_element_type=jnp.float32).astype(jnp.bfloat16)
            total = total + lax.optimization_barrier(part).astype(jnp.float32)
        return total.astype(jnp.bfloat16)
    gps = lax.map(backward, jnp.arange(BLOCKS, dtype=jnp.int32))
    loss = jnp.sum(losses) / jnp.sum(counts).astype(jnp.float32)
    return (loss, gqs.reshape(ROWS, D), gps.reshape(ROWS, D))
```

```python
import functools
import math

import jax
import jax.numpy as jnp
from jax import lax
from jax.experimental import pallas as pl
from jax.experimental.pallas import tpu as pltpu
from jax.sharding import PartitionSpec as P

WIN = 3
CHUNKS = 8
GROUP = 32
MESH = pl.DeviceIdType.MESH
ROWS_BY_ROWS = (((1,), (1,)), ((), ()))
COLS_BY_ROWS = (((0,), (0,)), ((), ()))


def kernel(ndp, nmp, inv, q_hbm, p_hbm, ps_ref, qs_ref, partners_ref, counts_ref,
           gq_ref, gp_ref, loss_ref,
           q_ref, p_ref, pbuf, qbuf, psown, psbuf, raw, inbox, weights, rw_out, rw_in, acc, lsum, lin,
           own_sem, p_ss, p_rs, q_ss, q_rs, sc_ss, sc_rs, t_ss, t_rs, k_ss, k_rs,
           d_ss, d_rs, g_ss, g_rs, l_ss, l_rs):
    d = lax.axis_index("dp")
    m = lax.axis_index("mp")
    rows, width = q_ref.shape
    share = rows // nmp
    step = rows // CHUNKS
    half = rows // 2
    first = CHUNKS // 2

    def at_dp(delta):
        return (lax.rem(d + delta + ndp, ndp), m)

    def flip(index, bit):
        return index + bit - 2 * bit * lax.rem(index // bit, 2)

    def rows_of(block):
        return pl.ds(pl.multiple_of(block * share, share), share)

    def half_of(h):
        return pl.ds(pl.multiple_of(h * half, half), half)

    even = lax.rem(d, 2) == 0
    odd = lax.rem(d, 2) == 1
    parity = lax.rem(d, 2)
    partner = (flip(d, 1), m)
    mp_bits = [1 << b for b in range(nmp.bit_length() - 1)]
    dp_bits = [1 << b for b in range(ndp.bit_length() - 1)]

    own_q = pltpu.make_async_copy(q_hbm, q_ref, own_sem.at[0])
    own_p = pltpu.make_async_copy(p_hbm, p_ref, own_sem.at[1])
    own_q.start()
    own_p.start()

    peers = [at_dp(s * k) for k in range(1, WIN + 1) for s in (1, -1)]
    peers += [(d, flip(m, b)) for b in mp_bits]
    peers += [(flip(d, b), m) for b in dp_bits if b > WIN]
    barrier = pltpu.get_barrier_semaphore()
    for peer in peers:
        pl.semaphore_signal(barrier, inc=1, device_id=peer, device_id_type=MESH)
    psown[...] = jnp.broadcast_to(ps_ref[...].astype(jnp.float32), psown.shape)
    pl.semaphore_wait(barrier, len(peers))

    def copy(src, dst, ssem, rsem, dev):
        return pltpu.make_async_remote_copy(
            src_ref=src, dst_ref=dst, send_sem=ssem, recv_sem=rsem,
            device_id=dev, device_id_type=MESH)

    class Stream:
        def __init__(self, own, buf, ss, rs, dest, far):
            self.own, self.buf, self.ss, self.rs, self.dest = own, buf, ss, rs, dest
            self.far, self.near = far, jnp.logical_not(far)

        def cut(self, c):
            return pl.ds(c * step, step)

        def move(self, kind, source, target, c, dev):
            s = self.cut(c)
            src = self.own.at[s] if source is None else self.buf.at[source, s]
            return copy(src, self.buf.at[target, s], self.ss.at[kind, c], self.rs.at[target, c], dev)

        def direct(self, c):
            return self.move(0, None, 1, c, self.dest)

        def across_own(self, c):
            return self.move(1, None, 0, c, partner)

        def across_one(self, c):
            return self.move(1, 1, 0, c, partner)

        def onward(self, c):
            return self.move(2, 0, 2, c, self.dest)

        def across_first(self, c):
            return self.move(3, 1, 2, c, partner)

        def across_second(self, c):
            return self.move(3, 2, 1, c, partner)

        def arrived(self, slot, c):
            s = self.cut(c)
            copy(self.buf.at[slot, s], self.buf.at[slot, s], self.ss.at[0, c], self.rs.at[slot, c], partner).wait_recv()

        def begin(self):
            @pl.when(self.far)
            def _():
                for c in range(CHUNKS):
                    self.across_own(c).start()
                    if c < first:
                        self.direct(c).start()

            @pl.when(self.near)
            def _():
                for c in range(CHUNKS):
                    self.direct(c).start()

        def relay(self, c):
            @pl.when(self.far)
            def _():
                if c < first:
                    self.arrived(1, c)
                    self.across_first(c).start()
                self.arrived(0, c)
                self.onward(c).start()

            @pl.when(self.near)
            def _():
                self.arrived(1, c)
                self.across_one(c).start()
                self.arrived(0, c)
                if c >= first:
                    self.onward(c).start()

        def early(self):
            @pl.when(self.far)
            def _():
                for c in range(first):
                    self.arrived(2, c)

        def relay_late(self, c):
            @pl.when(self.far)
            def _():
                self.arrived(1, c)

            @pl.when(self.near)
            def _():
                self.arrived(2, c)
                self.across_second(c).start()

        def late(self):
            @pl.when(self.far)
            def _():
                for c in range(first, CHUNKS):
                    self.arrived(2, c)

            @pl.when(self.near)
            def _():
                for c in range(first):
                    self.arrived(2, c)

        def finish(self):
            @pl.when(self.far)
            def _():
                for c in range(CHUNKS):
                    self.across_own(c).wait_send()
                    self.onward(c).wait_send()
                    if c < first:
                        self.direct(c).wait_send()
                        self.across_first(c).wait_send()

            @pl.when(self.near)
            def _():
                for c in range(CHUNKS):
                    self.direct(c).wait_send()
                    self.across_one(c).wait_send()
                    if c >= first:
                        self.onward(c).wait_send()
                        self.across_second(c).wait_send()

    ps = Stream(p_hbm, pbuf, p_ss, p_rs, at_dp(-2), odd)
    qs = Stream(q_hbm, qbuf, q_ss, q_rs, at_dp(2), even)

    def scale_copy(k):
        return copy(psown, psbuf.at[k - 1], sc_ss.at[k - 1], sc_rs.at[k - 1], at_dp(-k))

    ps.begin()
    for k in range(1, WIN + 1):
        scale_copy(k).start()

    def across(s):
        block = m
        for b in mp_bits:
            if s & b:
                block = flip(block, b)
        return rows_of(block)

    def tile_copy(k, h, s):
        return copy(raw.at[k, h, across(s)], inbox.at[s - 1, k, h],
                    t_ss.at[s - 1, k, h], t_rs.at[s - 1, k, h], (d, flip(m, s & -s)))

    def tile_next(k, h):
        for bit in mp_bits[1:]:
            for s in range(bit, nmp, 2 * bit):
                for b in mp_bits:
                    if b < bit:
                        tile_copy(k, h, s | b).wait_recv()
                        raw[k, h, across(s), :] += inbox[(s | b) - 1, k, h]
                tile_copy(k, h, s).start()

    def tile(k, h, keys):
        raw[k, h] = lax.dot_general(q_ref[...], keys, ROWS_BY_ROWS, preferred_element_type=jnp.float32)
        for s in range(1, nmp, 2):
            tile_copy(k, h, s).start()

    def tile_far(k, h):
        tile(k, h, pbuf[k - 1, half_of(h), :])

    own_q.wait()
    own_p.wait()
    for h in range(2):
        tile(0, h, p_ref[h * half:(h + 1) * half, :])
    ps.relay(0)
    for h in range(2):
        tile_next(0, h)
    for c in range(1, first):
        ps.relay(c)
    tile_far(2, 0)
    ps.relay(first)
    tile_next(2, 0)
    tile_far(1, 0)
    ps.relay(first + 1)
    tile_next(1, 0)
    for c in range(first + 2, CHUNKS):
        ps.relay(c)
    tile_far(1, 1)
    ps.early()
    tile_far(2 + parity, 1 - parity)
    tile_next(1, 1)
    tile_next(2 + parity, 1 - parity)
    for c in range(first, CHUNKS):
        ps.relay_late(c)
    qs.begin()
    tile_far(3 - parity, 1)
    ps.late()
    tile_far(3, parity)
    tile_next(3 - parity, 1)
    tile_next(3, parity)
    for k in range(1, WIN + 1):
        scale_copy(k).wait_recv()
    qs.relay(0)
    for k in range(WIN + 1):
        for h in range(2):
            for b in mp_bits:
                tile_copy(k, h, b).wait_recv()

    lsum[...] = jnp.zeros_like(lsum)
    live = [None] + [functools.reduce(jnp.logical_or, [partners_ref[0, j] == k for j in range(partners_ref.shape[1])])
                     for k in range(1, WIN + 1)]
    counted = [counts_ref[lax.rem(d + k, ndp)] for k in range(WIN + 1)]
    key_count = [counted[0]] + [jnp.where(live[k], counted[k], 0) for k in range(1, WIN + 1)]
    query_scale = qs_ref[...].astype(jnp.float32)

    @pl.loop(0, share // GROUP)
    def _(g):
        low = pl.multiple_of(g * GROUP, GROUP)
        here = pl.ds(low, GROUP)
        whole = pl.ds(pl.multiple_of(m * share + low, GROUP), GROUP)
        cols = lax.broadcasted_iota(jnp.int32, (GROUP, rows), 1)
        ids = lax.broadcasted_iota(jnp.int32, (GROUP, rows), 0) + (m * share + low)
        diagonal = cols == ids
        row_scale = jnp.sum(jnp.where(diagonal, query_scale, 0.0), axis=1, keepdims=True)
        valid = ids[:, 0:1] < key_count[0]
        key_scale = [psown[0:1, :]] + [psbuf[k, 0:1, :] for k in range(WIN)]
        scores = []
        for k in range(WIN + 1):
            parts = []
            for h in range(2):
                s = raw[k, h, whole, :]
                for b in mp_bits:
                    s = s + inbox[b - 1, k, h, here, :]
                parts.append(s)
            scores.append(jnp.concatenate(parts, axis=1) * (row_scale * inv) * key_scale[k])
        masked = [jnp.where(cols < key_count[k], scores[k], -jnp.inf) for k in range(WIN + 1)]
        top = functools.reduce(jnp.maximum, [jnp.max(x, axis=1, keepdims=True) for x in masked])
        exps = [jnp.exp(x - top) for x in masked]
        total = sum(jnp.sum(x, axis=1, keepdims=True) for x in exps)
        lse = top + jnp.log(total)
        positive = jnp.sum(jnp.where(diagonal, scores[0], 0.0), axis=1, keepdims=True)
        lost = jnp.sum(jnp.where(valid, lse - positive, 0.0), axis=0, keepdims=True)
        lsum[0] = lsum[0] + lost
        for k in range(WIN + 1):
            grad = exps[k] / total
            if k == 0:
                grad = grad - diagonal.astype(jnp.float32)
            grad = jnp.where(valid, grad, 0.0)
            weights[k, whole, :] = (grad * key_scale[k]).astype(jnp.bfloat16)
            if k == 0:
                weights[WIN + 1, whole, :] = (grad * row_scale).astype(jnp.bfloat16)
            else:
                rw_out[k - 1, here, :] = (grad * row_scale).astype(jnp.bfloat16)

    def dispatch(k):
        return copy(rw_out.at[k - 1], rw_in.at[k - 1, rows_of(m)], d_ss.at[k - 1], d_rs.at[k - 1], at_dp(k))

    for k in range(1, WIN + 1):
        dispatch(k).start()

    class Gather:
        def __init__(self, buf, ss, rs):
            self.buf, self.ss, self.rs = buf, ss, rs
            known = [0]
            self.steps = []
            for bit in reversed(mp_bits):
                self.steps += [(s, bit) for s in known]
                known = known + [s ^ bit for s in known]
            self.steps.sort(key=lambda t: t[0])
            self.got = set()

        def hop(self, s, bit):
            part = self.buf.at[:, across(s)]
            return copy(part, part, self.ss.at[s ^ bit], self.rs.at[s ^ bit], (d, flip(m, bit)))

        def take(self, s):
            if s and s not in self.got:
                self.got.add(s)
                part = self.buf.at[:, across(s)]
                copy(part, part, self.ss.at[s], self.rs.at[s], (d, flip(m, 1))).wait_recv()

        def begin(self):
            for s, bit in self.steps:
                if s == 0:
                    self.hop(s, bit).start()

        def rest(self):
            for s, bit in self.steps:
                if s:
                    self.take(s)
                    self.hop(s, bit).start()

        def all(self):
            for s in range(1, nmp):
                self.take(s)

        def finish(self):
            for s, bit in self.steps:
                self.hop(s, bit).wait_send()

    local = Gather(weights, k_ss, k_rs)
    foreign = Gather(rw_in, g_ss, g_rs)
    stages = [(d, flip(m, b)) for b in mp_bits] + [(flip(d, b), m) for b in dp_bits]

    def loss_copy(i):
        return copy(lsum.at[i], lin.at[i], l_ss.at[i], l_rs.at[i], stages[i])

    def loss_step(i):
        if i > len(stages):
            return
        if i:
            loss_copy(i - 1).wait_recv()
            lsum[i] = lsum[i - 1] + lin[i - 1]
        if i < len(stages):
            loss_copy(i).start()

    local.begin()
    loss_step(0)
    for c in range(1, first):
        qs.relay(c)
        loss_step(c)
    for k in range(1, WIN + 1):
        dispatch(k).wait_recv()
    foreign.begin()
    for c in range(first, CHUNKS):
        qs.relay(c)
        loss_step(c)
    local.rest()
    local.all()

    @pl.loop(0, nmp)
    def _(r):
        at = rows_of(r)
        out = jnp.dot(weights[0, at, :], p_ref[...], preferred_element_type=jnp.float32)
        for k in range(WIN):
            out = out + jnp.dot(weights[k + 1, at, :], pbuf[k], preferred_element_type=jnp.float32)
        gq_ref[at, :] = out.astype(jnp.bfloat16)

    foreign.rest()
    foreign.all()
    for i in range(CHUNKS, len(stages) + 1):
        loss_step(i)
    total_count = functools.reduce(lambda x, y: x + y, [counts_ref[i] for i in range(ndp)])
    loss_ref[...] = lsum[len(stages), 0:1, 0:1] / total_count.astype(jnp.float32)

    def back(w, x):
        return lax.dot_general(w, x, COLS_BY_ROWS, preferred_element_type=jnp.float32)

    qs.early()
    far = 1 - parity
    mid = (1 + far, half_of(1 - far))
    late_a = (2 - far, half_of(1))
    late_b = (2, half_of(far))

    for r in range(2):
        at = pl.ds(r * half, half)
        acc[at, :] = (back(weights[WIN + 1, :, at], q_ref[...]) + back(rw_in[0, :, at], qbuf[0])
                      + back(rw_in[1, 0:half, at], qbuf[1, 0:half, :])
                      + back(rw_in[mid[0], mid[1], at], qbuf[mid[0], mid[1], :]))
    for c in range(first, CHUNKS):
        qs.relay_late(c)
    for r in range(2):
        at = pl.ds(r * half, half)
        acc[at, :] = acc[at, :] + back(rw_in[late_a[0], late_a[1], at], qbuf[late_a[0], late_a[1], :])
    qs.late()
    for r in range(2):
        at = pl.ds(r * half, half)
        gp_ref[at, :] = (acc[at, :] + back(rw_in[late_b[0], late_b[1], at], qbuf[late_b[0], late_b[1], :])
                         ).astype(jnp.bfloat16)

    ps.finish()
    qs.finish()
    for k in range(1, WIN + 1):
        scale_copy(k).wait_send()
        dispatch(k).wait_send()
    for k in range(WIN + 1):
        for h in range(2):
            for j in range(1, nmp):
                tile_copy(k, h, j).wait_send()
    local.finish()
    foreign.finish()
    for i in range(len(stages)):
        loss_copy(i).wait_send()


def local(ndp, nmp, query, passage, query_scale, passage_scale, partners, counts):
    rows, width = query.shape
    inv = 1.0 / math.sqrt(width * nmp)
    share = rows // nmp
    nst = (ndp * nmp).bit_length() - 1
    bf, f32 = jnp.bfloat16, jnp.float32
    dma = pltpu.SemaphoreType.DMA
    vm = pl.BlockSpec(memory_space=pltpu.VMEM)
    sm = pl.BlockSpec(memory_space=pltpu.SMEM)
    hbm = pl.BlockSpec(memory_space=pl.ANY)
    gq, gp, loss = pl.pallas_call(
        functools.partial(kernel, ndp, nmp, inv),
        out_shape=[
            jax.ShapeDtypeStruct((rows, width), bf),
            jax.ShapeDtypeStruct((rows, width), bf),
            jax.ShapeDtypeStruct((1, 1), f32),
        ],
        in_specs=[hbm, hbm, vm, vm, sm, sm],
        out_specs=[vm] * 3,
        scratch_shapes=[
            pltpu.VMEM((rows, width), bf),
            pltpu.VMEM((rows, width), bf),
            pltpu.VMEM((WIN, rows, width), bf),
            pltpu.VMEM((WIN, rows, width), bf),
            pltpu.VMEM((8, rows), f32),
            pltpu.VMEM((WIN, 8, rows), f32),
            pltpu.VMEM((WIN + 1, 2, rows, rows // 2), f32),
            pltpu.VMEM((nmp - 1, WIN + 1, 2, share, rows // 2), f32),
            pltpu.VMEM((WIN + 2, rows, rows), bf),
            pltpu.VMEM((WIN, share, rows), bf),
            pltpu.VMEM((WIN, rows, rows), bf),
            pltpu.VMEM((rows, width), f32),
            pltpu.VMEM((nst + 1, 8, 128), f32),
            pltpu.VMEM((nst, 8, 128), f32),
            dma((2,)),
            dma((4, CHUNKS)), dma((WIN, CHUNKS)),
            dma((4, CHUNKS)), dma((WIN, CHUNKS)),
            dma((WIN,)), dma((WIN,)),
            dma((nmp - 1, WIN + 1, 2)), dma((nmp - 1, WIN + 1, 2)),
            dma((nmp,)), dma((nmp,)),
            dma((WIN,)), dma((WIN,)),
            dma((nmp,)), dma((nmp,)),
            dma((nst,)), dma((nst,)),
        ],
        compiler_params=pltpu.CompilerParams(
            collective_id=0, has_side_effects=True, vmem_limit_bytes=48 * 1024 * 1024),
    )(query, passage, passage_scale[None, :], query_scale[None, :], partners, counts)
    return loss.reshape(()), gq, gp


def solution(mesh):
    return jax.shard_map(
        functools.partial(local, mesh.shape["dp"], mesh.shape["mp"]),
        mesh=mesh,
        in_specs=(P("dp", "mp"), P("dp", "mp"), P("dp"), P("dp"), P("dp", None), P()),
        out_specs=(P(), P("dp", "mp"), P("dp", "mp")),
        check_vma=False,
    )
```

```python
import functools
import math

import jax
import jax.numpy as jnp
from jax import lax
from jax.experimental import pallas as pl
from jax.experimental.pallas import tpu as pltpu
from jax.sharding import PartitionSpec as P

WIN = 3
CHUNKS = 8
FIRST = 5
GROUP = 32
MESH = pl.DeviceIdType.MESH
ROWS_BY_ROWS = (((1,), (1,)), ((), ()))
COLS_BY_ROWS = (((0,), (0,)), ((), ()))


def kernel(ndp, nmp, inv, q_hbm, p_hbm, ps_hbm, qs_hbm, partners_hbm, counts_hbm,
           gq_ref, gp_ref, loss_ref,
           q_ref, p_ref, ps_ref, qs_ref, partners_ref, counts_ref, pbuf, qbuf, psown, psbuf, raw, inbox, weights, rw_out, rw_in, acc, lsum, lin,
           own_sem, p_ss, p_rs, q_ss, q_rs, t_ss, t_rs, k_ss, k_rs,
           d_ss, d_rs, g_ss, g_rs, l_ss, l_rs):
    d = lax.axis_index("dp")
    m = lax.axis_index("mp")
    rows, width = q_ref.shape
    share = rows // nmp
    step = rows // CHUNKS
    half = rows // 2
    first = FIRST
    middle = CHUNKS // 2

    def at_dp(delta):
        return (lax.rem(d + delta + ndp, ndp), m)

    def flip(index, bit):
        return index + bit - 2 * bit * lax.rem(index // bit, 2)

    def flip_all(index, bits):
        for b in (1 << i for i in range(bits.bit_length())):
            if bits & b:
                index = flip(index, b)
        return index

    def rows_of(block):
        return pl.ds(pl.multiple_of(block * share, share), share)

    def half_of(h):
        return pl.ds(pl.multiple_of(h * half, half), half)

    even = lax.rem(d, 2) == 0
    odd = lax.rem(d, 2) == 1
    parity = lax.rem(d, 2)
    partner = (flip(d, 1), m)
    mp_bits = [1 << b for b in range(nmp.bit_length() - 1)]
    dp_bits = [1 << b for b in range(ndp.bit_length() - 1)]

    small = [(ps_hbm, ps_ref), (qs_hbm, qs_ref), (partners_hbm, partners_ref), (counts_hbm, counts_ref)]
    small = [pltpu.make_async_copy(src, dst, own_sem.at[2 + i]) for i, (src, dst) in enumerate(small)]
    own_q = pltpu.make_async_copy(q_hbm, q_ref, own_sem.at[0])
    own_p = pltpu.make_async_copy(p_hbm, p_ref, own_sem.at[1])

    peers = [partner, at_dp(2), at_dp(-2)]
    peers += [(d, flip(m, b)) for b in mp_bits]
    peers += [(flip(d, b), m) for b in dp_bits if b > WIN + 1]
    barrier = pltpu.get_barrier_semaphore()
    for peer in peers:
        pl.semaphore_signal(barrier, inc=1, device_id=peer, device_id_type=MESH)
    for c in small:
        c.start()
    own_q.start()
    own_p.start()
    small[0].wait()
    psown[...] = jnp.broadcast_to(ps_ref[...].astype(jnp.float32)[None, :], psown.shape)
    pl.semaphore_wait(barrier, len(peers))

    def copy(src, dst, ssem, rsem, dev):
        return pltpu.make_async_remote_copy(
            src_ref=src, dst_ref=dst, send_sem=ssem, recv_sem=rsem,
            device_id=dev, device_id_type=MESH)

    class Stream:
        def __init__(self, own, buf, ss, rs, dest, far, extra=None):
            self.own, self.buf, self.ss, self.rs, self.dest = own, buf, ss, rs, dest
            self.far, self.near, self.extra = far, jnp.logical_not(far), extra
            self.order = ([] if extra is None else [-1]) + list(range(CHUNKS))

        def cut(self, slot, c):
            own, buf = (self.own, self.buf) if c >= 0 else self.extra
            at = pl.ds(max(c, 0) * step, step if c >= 0 else own.shape[0])
            return own.at[at] if slot is None else buf.at[slot, at]

        def move(self, kind, source, target, c, dev):
            return copy(self.cut(source, c), self.cut(target, c),
                        self.ss.at[kind, c % (CHUNKS + 1)], self.rs.at[target, c % (CHUNKS + 1)], dev)

        def direct(self, c):
            return self.move(0, None, 1, c, self.dest)

        def across_own(self, c):
            return self.move(1, None, 0, c, partner)

        def across_one(self, c):
            return self.move(1, 1, 0, c, partner)

        def onward(self, c):
            return self.move(2, 0, 2, c, self.dest)

        def across_first(self, c):
            return self.move(3, 1, 2, c, partner)

        def across_second(self, c):
            return self.move(3, 2, 1, c, partner)

        def arrived(self, slot, c):
            self.move(0, slot, slot, c, partner).wait_recv()

        def begin(self):
            @pl.when(self.far)
            def _():
                for c in self.order:
                    self.across_own(c).start()
                    if c < first:
                        self.direct(c).start()

            @pl.when(self.near)
            def _():
                for c in self.order:
                    self.direct(c).start()

        def relay(self, c):
            @pl.when(self.far)
            def _():
                if c < first:
                    self.arrived(1, c)
                    self.across_first(c).start()
                self.arrived(0, c)
                self.onward(c).start()

            @pl.when(self.near)
            def _():
                self.arrived(1, c)
                self.across_one(c).start()
                self.arrived(0, c)
                if c >= first:
                    self.onward(c).start()

        def early(self):
            @pl.when(self.far)
            def _():
                for c in range(middle):
                    self.arrived(2, c)

        def relay_late(self, c):
            @pl.when(self.far)
            def _():
                self.arrived(1, c)

            @pl.when(self.near)
            def _():
                self.arrived(2, c)
                self.across_second(c).start()

        def late(self):
            @pl.when(self.near)
            def _():
                for c in range(middle):
                    self.arrived(2, c)

        def last(self):
            @pl.when(self.far)
            def _():
                for c in range(middle, CHUNKS):
                    self.arrived(2, c)

            @pl.when(self.near)
            def _():
                for c in range(middle, first):
                    self.arrived(2, c)

        def last_extra(self):
            self.arrived(2, -1)

        def finish(self):
            @pl.when(self.far)
            def _():
                for c in self.order:
                    self.across_own(c).wait_send()
                    self.onward(c).wait_send()
                    if c < first:
                        self.direct(c).wait_send()
                        self.across_first(c).wait_send()

            @pl.when(self.near)
            def _():
                for c in self.order:
                    self.direct(c).wait_send()
                    self.across_one(c).wait_send()
                    if c >= first:
                        self.onward(c).wait_send()
                        self.across_second(c).wait_send()

    ps = Stream(p_hbm, pbuf, p_ss, p_rs, at_dp(-2), odd, (psown, psbuf))
    qs = Stream(q_hbm, qbuf, q_ss, q_rs, at_dp(2), even)

    ps.begin()

    def across(s):
        block = m
        for b in mp_bits:
            if s & b:
                block = flip(block, b)
        return rows_of(block)

    def tile_copy(k, h, s):
        return copy(raw.at[k, h, across(s)], inbox.at[s - 1, k, h],
                    t_ss.at[s - 1, k, h], t_rs.at[s - 1, k, h], (d, flip(m, s & -s)))

    def tile_next(k, h):
        for bit in mp_bits[1:]:
            for s in range(bit, nmp, 2 * bit):
                for b in mp_bits:
                    if b < bit:
                        tile_copy(k, h, s | b).wait_recv()
                        raw[k, h, across(s), :] += inbox[(s | b) - 1, k, h]
                tile_copy(k, h, s).start()

    def tile(k, h, keys):
        raw[k, h] = lax.dot_general(q_ref[...], keys, ROWS_BY_ROWS, preferred_element_type=jnp.float32)
        for s in range(1, nmp, 2):
            tile_copy(k, h, s).start()

    def tile_far(k, h):
        tile(k, h, pbuf[k - 1, half_of(h), :])

    own_q.wait()
    own_p.wait()
    for h in range(2):
        tile(0, h, p_ref[h * half:(h + 1) * half, :])
    ps.relay(-1)
    ps.relay(0)
    for h in range(2):
        tile_next(0, h)
    for c in range(1, middle):
        ps.relay(c)
    tile_far(2, 0)
    ps.relay(middle)
    tile_next(2, 0)
    tile_far(1, 0)
    ps.relay(middle + 1)
    tile_next(1, 0)
    for c in range(middle + 2, CHUNKS):
        ps.relay(c)
    tile_far(1, 1)
    ps.early()
    tile_far(2 + parity, 1 - parity)
    tile_next(1, 1)
    tile_next(2 + parity, 1 - parity)
    for c in range(first, CHUNKS):
        ps.relay_late(c)
    qs.begin()
    ps.late()
    tile_far(3 - parity, parity)
    ps.last()
    tile_far(3, 1)
    tile_next(3 - parity, parity)
    tile_next(3, 1)
    ps.last_extra()
    qs.relay(0)
    for c in small[1:]:
        c.wait()
    for k in range(WIN + 1):
        for h in range(2):
            for b in mp_bits:
                tile_copy(k, h, b).wait_recv()

    lsum[...] = jnp.zeros_like(lsum)
    live = [None] + [functools.reduce(jnp.logical_or, [partners_ref[0, j] == k for j in range(partners_ref.shape[1])])
                     for k in range(1, WIN + 1)]
    counted = [counts_ref[lax.rem(d + k, ndp)] for k in range(WIN + 1)]
    key_count = [counted[0]] + [jnp.where(live[k], counted[k], 0) for k in range(1, WIN + 1)]
    query_scale = qs_ref[...].astype(jnp.float32)[None, :]

    @pl.loop(0, share // GROUP)
    def _(g):
        low = pl.multiple_of(g * GROUP, GROUP)
        here = pl.ds(low, GROUP)
        whole = pl.ds(pl.multiple_of(m * share + low, GROUP), GROUP)
        cols = lax.broadcasted_iota(jnp.int32, (GROUP, rows), 1)
        ids = lax.broadcasted_iota(jnp.int32, (GROUP, rows), 0) + (m * share + low)
        diagonal = cols == ids
        row_scale = jnp.sum(jnp.where(diagonal, query_scale, 0.0), axis=1, keepdims=True)
        valid = ids[:, 0:1] < key_count[0]
        key_scale = [psown[0:1, :]] + [psbuf[k, 0:1, :] for k in range(WIN)]
        scores = []
        for k in range(WIN + 1):
            parts = []
            for h in range(2):
                s = raw[k, h, whole, :]
                for b in mp_bits:
                    s = s + inbox[b - 1, k, h, here, :]
                parts.append(s)
            scores.append(jnp.concatenate(parts, axis=1) * (row_scale * inv) * key_scale[k])
        masked = [jnp.where(cols < key_count[k], scores[k], -jnp.inf) for k in range(WIN + 1)]
        top = functools.reduce(jnp.maximum, [jnp.max(x, axis=1, keepdims=True) for x in masked])
        exps = [jnp.exp(x - top) for x in masked]
        total = sum(jnp.sum(x, axis=1, keepdims=True) for x in exps)
        lse = top + jnp.log(total)
        positive = jnp.sum(jnp.where(diagonal, scores[0], 0.0), axis=1, keepdims=True)
        lost = jnp.sum(jnp.where(valid, lse - positive, 0.0), axis=0, keepdims=True)
        lsum[0] = lsum[0] + lost
        for k in range(WIN + 1):
            grad = exps[k] / total
            if k == 0:
                grad = grad - diagonal.astype(jnp.float32)
            grad = jnp.where(valid, grad, 0.0)
            weights[k, whole, :] = (grad * key_scale[k]).astype(jnp.bfloat16)
            if k == 0:
                weights[WIN + 1, whole, :] = (grad * row_scale).astype(jnp.bfloat16)
            else:
                rw_out[k - 1, here, :] = (grad * row_scale).astype(jnp.bfloat16)

    def dispatch(k):
        return copy(rw_out.at[k - 1], rw_in.at[k - 1, rows_of(m)], d_ss.at[k - 1], d_rs.at[k - 1], at_dp(k))

    for k in range(1, WIN + 1):
        dispatch(k).start()

    class Gather:
        def __init__(self, buf, ss, rs):
            self.buf, self.ss, self.rs = buf, ss, rs
            known = [0]
            self.steps = []
            for bit in reversed(mp_bits):
                self.steps += [(s, bit) for s in known]
                known = known + [s ^ bit for s in known]
            self.steps.sort(key=lambda t: t[0])
            self.got = set()

        def hop(self, s, bit):
            part = self.buf.at[:, across(s)]
            return copy(part, part, self.ss.at[s ^ bit], self.rs.at[s ^ bit], (d, flip(m, bit)))

        def take(self, s):
            if s and s not in self.got:
                self.got.add(s)
                part = self.buf.at[:, across(s)]
                copy(part, part, self.ss.at[s], self.rs.at[s], (d, flip(m, 1))).wait_recv()

        def begin(self):
            for s, bit in self.steps:
                if s == 0:
                    self.hop(s, bit).start()

        def rest(self):
            for s, bit in self.steps:
                if s:
                    self.take(s)
                    self.hop(s, bit).start()

        def all(self):
            for s in range(1, nmp):
                self.take(s)

        def finish(self):
            for s, bit in self.steps:
                self.hop(s, bit).wait_send()

    local = Gather(weights, k_ss, k_rs)
    foreign = Gather(rw_in, g_ss, g_rs)
    stages = []
    for bits, peer in ((mp_bits, lambda o: (d, flip_all(m, o))), (dp_bits, lambda o: (flip_all(d, o), m))):
        for i in range(0, len(bits), 2):
            pair = bits[i:i + 2]
            stages.append([peer(sum(pair[:1]))] if len(pair) == 1 else [peer(o) for o in (*pair, sum(pair))])

    def loss_copies(i):
        return [copy(lsum.at[i], lin.at[i, j], l_ss.at[i, j], l_rs.at[i, j], dev) for j, dev in enumerate(stages[i])]

    def loss_step(i):
        if i:
            for j, c in enumerate(loss_copies(i - 1)):
                c.wait_recv()
            lsum[i] = functools.reduce(lambda x, y: x + y, [lin[i - 1, j] for j in range(len(stages[i - 1]))], lsum[i - 1])
        if i < len(stages):
            for c in loss_copies(i):
                c.start()

    local.begin()
    loss_step(0)
    for c in range(1, CHUNKS):
        qs.relay(c)
    for k in range(1, WIN + 1):
        dispatch(k).wait_recv()
    foreign.begin()
    local.rest()
    loss_step(1)
    local.all()

    @pl.loop(0, nmp)
    def _(r):
        at = rows_of(r)
        out = jnp.dot(weights[0, at, :], p_ref[...], preferred_element_type=jnp.float32)
        for k in range(WIN):
            out = out + jnp.dot(weights[k + 1, at, :], pbuf[k], preferred_element_type=jnp.float32)
        gq_ref[at, :] = out.astype(jnp.bfloat16)

    foreign.rest()
    foreign.all()

    def back(w, x):
        return lax.dot_general(w, x, COLS_BY_ROWS, preferred_element_type=jnp.float32)

    qs.early()
    far = 1 - parity
    mid = (1 + far, half_of(1 - far))
    late_a = (2 - far, half_of(far))

    for r in range(2):
        at = pl.ds(r * half, half)
        acc[at, :] = (back(weights[WIN + 1, :, at], q_ref[...]) + back(rw_in[0, :, at], qbuf[0])
                      + back(rw_in[1, 0:half, at], qbuf[1, 0:half, :])
                      + back(rw_in[mid[0], mid[1], at], qbuf[mid[0], mid[1], :]))
    for i in range(2, len(stages)):
        loss_step(i)
    for c in range(first, CHUNKS):
        qs.relay_late(c)
    qs.late()
    for r in range(2):
        at = pl.ds(r * half, half)
        acc[at, :] = acc[at, :] + back(rw_in[late_a[0], late_a[1], at], qbuf[late_a[0], late_a[1], :])
    loss_step(len(stages))
    total_count = functools.reduce(lambda x, y: x + y, [counts_ref[i] for i in range(ndp)])
    loss_ref[...] = lsum[len(stages), 0:1, 0:1] / total_count.astype(jnp.float32)
    qs.last()
    for r in range(2):
        at = pl.ds(r * half, half)
        gp_ref[at, :] = (acc[at, :] + back(rw_in[2, half:rows, at], qbuf[2, half:rows, :])).astype(jnp.bfloat16)

    ps.finish()
    qs.finish()
    for k in range(1, WIN + 1):
        dispatch(k).wait_send()
    for k in range(WIN + 1):
        for h in range(2):
            for j in range(1, nmp):
                tile_copy(k, h, j).wait_send()
    local.finish()
    foreign.finish()
    for i in range(len(stages)):
        for c in loss_copies(i):
            c.wait_send()


def local(ndp, nmp, query, passage, query_scale, passage_scale, partners, counts):
    rows, width = query.shape
    inv = 1.0 / math.sqrt(width * nmp)
    share = rows // nmp
    nst = sum(n.bit_length() // 2 for n in (ndp, nmp))
    bf, f32 = jnp.bfloat16, jnp.float32
    dma = pltpu.SemaphoreType.DMA
    vm = pl.BlockSpec(memory_space=pltpu.VMEM)
    hbm = pl.BlockSpec(memory_space=pltpu.HBM)
    gq, gp, loss = pl.pallas_call(
        functools.partial(kernel, ndp, nmp, inv),
        out_shape=[
            jax.ShapeDtypeStruct((rows, width), bf),
            jax.ShapeDtypeStruct((rows, width), bf),
            jax.ShapeDtypeStruct((1, 1), f32),
        ],
        in_specs=[hbm] * 6,
        out_specs=[vm] * 3,
        scratch_shapes=[
            pltpu.VMEM((rows, width), bf),
            pltpu.VMEM((rows, width), bf),
            pltpu.VMEM((rows,), bf),
            pltpu.VMEM((rows,), bf),
            pltpu.SMEM(partners.shape, jnp.int32),
            pltpu.SMEM(counts.shape, jnp.int32),
            pltpu.VMEM((WIN, rows, width), bf),
            pltpu.VMEM((WIN, rows, width), bf),
            pltpu.VMEM((8, rows), f32),
            pltpu.VMEM((WIN, 8, rows), f32),
            pltpu.VMEM((WIN + 1, 2, rows, rows // 2), f32),
            pltpu.VMEM((nmp - 1, WIN + 1, 2, share, rows // 2), f32),
            pltpu.VMEM((WIN + 2, rows, rows), bf),
            pltpu.VMEM((WIN, share, rows), bf),
            pltpu.VMEM((WIN, rows, rows), bf),
            pltpu.VMEM((rows, width), f32),
            pltpu.VMEM((nst + 1, 8, 128), f32),
            pltpu.VMEM((nst, 3, 8, 128), f32),
            dma((6,)),
            dma((4, CHUNKS + 1)), dma((WIN, CHUNKS + 1)),
            dma((4, CHUNKS + 1)), dma((WIN, CHUNKS + 1)),
            dma((nmp - 1, WIN + 1, 2)), dma((nmp - 1, WIN + 1, 2)),
            dma((nmp,)), dma((nmp,)),
            dma((WIN,)), dma((WIN,)),
            dma((nmp,)), dma((nmp,)),
            dma((nst, 3)), dma((nst, 3)),
        ],
        compiler_params=pltpu.CompilerParams(
            collective_id=0, has_side_effects=True, vmem_limit_bytes=48 * 1024 * 1024),
    )(*[pltpu.with_memory_space_constraint(x, pltpu.HBM)
        for x in (query, passage, passage_scale, query_scale, partners, counts)])
    return loss.reshape(()), gq, gp


def solution(mesh):
    return jax.shard_map(
        functools.partial(local, mesh.shape["dp"], mesh.shape["mp"]),
        mesh=mesh,
        in_specs=(P("dp", "mp"), P("dp", "mp"), P("dp"), P("dp"), P("dp", None), P()),
        out_specs=(P(), P("dp", "mp"), P("dp", "mp")),
        check_vma=False,
    )
```

```python
import functools
import math

import jax
import jax.numpy as jnp
from jax import lax
from jax.experimental import pallas as pl
from jax.experimental.pallas import tpu as pltpu
from jax.sharding import PartitionSpec as P

WIN = 3
CHUNKS = 8
FIRST = 5
AHEAD = 4
GROUP = 32
MESH = pl.DeviceIdType.MESH
ROWS_BY_ROWS = (((1,), (1,)), ((), ()))
COLS_BY_ROWS = (((0,), (0,)), ((), ()))


def kernel(ndp, nmp, inv, q_hbm, p_hbm, ps_hbm, qs_hbm, partners_hbm, counts_hbm,
           gq_ref, gp_ref, loss_ref,
           q_ref, p_ref, ps_ref, qs_ref, partners_ref, counts_ref, pbuf, qbuf, psown, psbuf, raw, inbox, weights, rw_out, rw_in, acc, lsum, lin,
           own_sem, p_ss, p_rs, q_ss, q_rs, t_ss, t_rs, k_ss, k_rs,
           d_ss, d_rs, g_ss, g_rs, l_ss, l_rs):
    d = lax.axis_index("dp")
    m = lax.axis_index("mp")
    rows, width = q_ref.shape
    share = rows // nmp
    step = rows // CHUNKS
    half = rows // 2
    first = FIRST
    middle = CHUNKS // 2

    def at_dp(delta):
        return (lax.rem(d + delta + ndp, ndp), m)

    def flip(index, bit):
        return index + bit - 2 * bit * lax.rem(index // bit, 2)

    def flip_all(index, bits):
        for b in (1 << i for i in range(bits.bit_length())):
            if bits & b:
                index = flip(index, b)
        return index

    def rows_of(block):
        return pl.ds(pl.multiple_of(block * share, share), share)

    def half_of(h):
        return pl.ds(pl.multiple_of(h * half, half), half)

    even = lax.rem(d, 2) == 0
    odd = lax.rem(d, 2) == 1
    parity = lax.rem(d, 2)
    partner = (flip(d, 1), m)
    mp_bits = [1 << b for b in range(nmp.bit_length() - 1)]
    dp_bits = [1 << b for b in range(ndp.bit_length() - 1)]

    small = [(ps_hbm, ps_ref), (qs_hbm, qs_ref), (partners_hbm, partners_ref), (counts_hbm, counts_ref)]
    small = [pltpu.make_async_copy(src, dst, own_sem.at[2 + i]) for i, (src, dst) in enumerate(small)]
    own_q = pltpu.make_async_copy(q_hbm, q_ref, own_sem.at[0])
    own_p = pltpu.make_async_copy(p_hbm, p_ref, own_sem.at[1])

    peers = [partner, at_dp(2), at_dp(-2)]
    peers += [(d, flip(m, b)) for b in mp_bits]
    peers += [(flip(d, b), m) for b in dp_bits if b > WIN + 1]
    barrier = pltpu.get_barrier_semaphore()
    for peer in peers:
        pl.semaphore_signal(barrier, inc=1, device_id=peer, device_id_type=MESH)
    for c in small:
        c.start()
    own_q.start()
    own_p.start()
    small[0].wait()
    psown[...] = jnp.broadcast_to(ps_ref[...].astype(jnp.float32)[None, :], psown.shape)
    pl.semaphore_wait(barrier, len(peers))

    def copy(src, dst, ssem, rsem, dev):
        return pltpu.make_async_remote_copy(
            src_ref=src, dst_ref=dst, send_sem=ssem, recv_sem=rsem,
            device_id=dev, device_id_type=MESH)

    class Stream:
        def __init__(self, own, buf, ss, rs, dest, far, extra=None):
            self.own, self.buf, self.ss, self.rs, self.dest = own, buf, ss, rs, dest
            self.far, self.near, self.extra = far, jnp.logical_not(far), extra
            self.order = ([] if extra is None else [-1]) + list(range(CHUNKS))

        def cut(self, slot, c):
            own, buf = (self.own, self.buf) if c >= 0 else self.extra
            at = pl.ds(max(c, 0) * step, step if c >= 0 else own.shape[0])
            return own.at[at] if slot is None else buf.at[slot, at]

        def move(self, kind, source, target, c, dev):
            return copy(self.cut(source, c), self.cut(target, c),
                        self.ss.at[kind, c % (CHUNKS + 1)], self.rs.at[target, c % (CHUNKS + 1)], dev)

        def direct(self, c):
            return self.move(0, None, 1, c, self.dest)

        def across_own(self, c):
            return self.move(1, None, 0, c, partner)

        def across_one(self, c):
            return self.move(1, 1, 0, c, partner)

        def onward(self, c):
            return self.move(2, 0, 2, c, self.dest)

        def across_first(self, c):
            return self.move(3, 1, 2, c, partner)

        def across_second(self, c):
            return self.move(3, 2, 1, c, partner)

        def arrived(self, slot, c):
            self.move(0, slot, slot, c, partner).wait_recv()

        def begin_direct(self, far, order):
            @pl.when(self.far if far else self.near)
            def _():
                for c in order:
                    if c < first or not far:
                        self.direct(c).start()

        def begin_across(self, order):
            @pl.when(self.far)
            def _():
                for c in order:
                    self.across_own(c).start()

        def begin(self, order):
            @pl.when(self.far)
            def _():
                for c in order:
                    self.across_own(c).start()
                    if c < first:
                        self.direct(c).start()

            @pl.when(self.near)
            def _():
                for c in order:
                    self.direct(c).start()

        def relay(self, c):
            @pl.when(self.far)
            def _():
                if c < first:
                    self.arrived(1, c)
                    self.across_first(c).start()
                self.arrived(0, c)
                self.onward(c).start()

            @pl.when(self.near)
            def _():
                self.arrived(1, c)
                self.across_one(c).start()
                self.arrived(0, c)
                if c >= first:
                    self.onward(c).start()

        def early(self):
            @pl.when(self.far)
            def _():
                for c in range(middle):
                    self.arrived(2, c)

        def relay_late(self, c):
            @pl.when(self.far)
            def _():
                self.arrived(1, c)

            @pl.when(self.near)
            def _():
                self.arrived(2, c)
                self.across_second(c).start()

        def late(self):
            @pl.when(self.near)
            def _():
                for c in range(middle):
                    self.arrived(2, c)

        def last(self):
            @pl.when(self.far)
            def _():
                for c in range(middle, CHUNKS):
                    self.arrived(2, c)

            @pl.when(self.near)
            def _():
                for c in range(middle, first):
                    self.arrived(2, c)

        def last_extra(self):
            self.arrived(2, -1)

        def finish(self):
            @pl.when(self.far)
            def _():
                for c in self.order:
                    self.across_own(c).wait_send()
                    self.onward(c).wait_send()
                    if c < first:
                        self.direct(c).wait_send()
                        self.across_first(c).wait_send()

            @pl.when(self.near)
            def _():
                for c in self.order:
                    self.direct(c).wait_send()
                    self.across_one(c).wait_send()
                    if c >= first:
                        self.onward(c).wait_send()
                        self.across_second(c).wait_send()

    ps = Stream(p_hbm, pbuf, p_ss, p_rs, at_dp(-2), odd, (psown, psbuf))
    qs = Stream(q_hbm, qbuf, q_ss, q_rs, at_dp(2), even)

    ps.begin(ps.order)

    def across(s):
        block = m
        for b in mp_bits:
            if s & b:
                block = flip(block, b)
        return rows_of(block)

    def tile_copy(k, h, s):
        return copy(raw.at[k, h, across(s)], inbox.at[s - 1, k, h],
                    t_ss.at[s - 1, k, h], t_rs.at[s - 1, k, h], (d, flip(m, s & -s)))

    def tile_next(k, h):
        for bit in mp_bits[1:]:
            for s in range(bit, nmp, 2 * bit):
                for b in mp_bits:
                    if b < bit:
                        tile_copy(k, h, s | b).wait_recv()
                        raw[k, h, across(s), :] += inbox[(s | b) - 1, k, h]
                tile_copy(k, h, s).start()

    def tile(k, h, keys):
        raw[k, h] = lax.dot_general(q_ref[...], keys, ROWS_BY_ROWS, preferred_element_type=jnp.float32)
        for s in range(1, nmp, 2):
            tile_copy(k, h, s).start()

    def tile_far(k, h):
        tile(k, h, pbuf[k - 1, half_of(h), :])

    own_q.wait()
    own_p.wait()
    for h in range(2):
        tile(0, h, p_ref[h * half:(h + 1) * half, :])
    ps.relay(-1)
    ps.relay(0)
    for h in range(2):
        tile_next(0, h)
    for c in range(1, middle):
        ps.relay(c)
    tile_far(2, 0)
    ps.relay(middle)
    tile_next(2, 0)
    tile_far(1, 0)
    ps.relay(middle + 1)
    tile_next(1, 0)
    for c in range(middle + 2, CHUNKS):
        ps.relay(c)
    qs.begin_direct(True, range(5))
    tile_far(1, 1)
    ps.early()
    tile_far(2 + parity, 1 - parity)
    tile_next(1, 1)
    tile_next(2 + parity, 1 - parity)
    qs.begin_direct(False, range(0))
    for c in range(first, CHUNKS):
        ps.relay_late(c)
        if c == first: qs.begin_direct(False, range(0, 2))
    qs.begin_across(range(CHUNKS))
    qs.begin_direct(False, range(2,CHUNKS))
    qs.begin_direct(True, range(5,CHUNKS))
    ps.late()
    tile_far(3 - parity, parity)
    ps.last()
    tile_far(3, 1)
    tile_next(3 - parity, parity)
    tile_next(3, 1)
    ps.last_extra()
    for c in range(2):
        qs.relay(c)
    for c in small[1:]:
        c.wait()
    for k in range(WIN + 1):
        for h in range(2):
            for b in mp_bits:
                tile_copy(k, h, b).wait_recv()

    lsum[...] = jnp.zeros_like(lsum)
    live = [None] + [functools.reduce(jnp.logical_or, [partners_ref[0, j] == k for j in range(partners_ref.shape[1])])
                     for k in range(1, WIN + 1)]
    counted = [counts_ref[lax.rem(d + k, ndp)] for k in range(WIN + 1)]
    key_count = [counted[0]] + [jnp.where(live[k], counted[k], 0) for k in range(1, WIN + 1)]
    query_scale = qs_ref[...].astype(jnp.float32)[None, :]

    @pl.loop(0, share // GROUP)
    def _(g):
        low = pl.multiple_of(g * GROUP, GROUP)
        here = pl.ds(low, GROUP)
        whole = pl.ds(pl.multiple_of(m * share + low, GROUP), GROUP)
        cols = lax.broadcasted_iota(jnp.int32, (GROUP, rows), 1)
        ids = lax.broadcasted_iota(jnp.int32, (GROUP, rows), 0) + (m * share + low)
        diagonal = cols == ids
        row_scale = jnp.sum(jnp.where(diagonal, query_scale, 0.0), axis=1, keepdims=True)
        valid = ids[:, 0:1] < key_count[0]
        key_scale = [psown[0:1, :]] + [psbuf[k, 0:1, :] for k in range(WIN)]
        scores = []
        for k in range(WIN + 1):
            parts = []
            for h in range(2):
                s = raw[k, h, whole, :]
                for b in mp_bits:
                    s = s + inbox[b - 1, k, h, here, :]
                parts.append(s)
            scores.append(jnp.concatenate(parts, axis=1) * (row_scale * inv) * key_scale[k])
        masked = [jnp.where(cols < key_count[k], scores[k], -jnp.inf) for k in range(WIN + 1)]
        top = functools.reduce(jnp.maximum, [jnp.max(x, axis=1, keepdims=True) for x in masked])
        exps = [jnp.exp(x - top) for x in masked]
        total = sum(jnp.sum(x, axis=1, keepdims=True) for x in exps)
        lse = top + jnp.log(total)
        positive = jnp.sum(jnp.where(diagonal, scores[0], 0.0), axis=1, keepdims=True)
        lost = jnp.sum(jnp.where(valid, lse - positive, 0.0), axis=0, keepdims=True)
        lsum[0] = lsum[0] + lost
        for k in range(WIN + 1):
            grad = exps[k] / total
            if k == 0:
                grad = grad - diagonal.astype(jnp.float32)
            grad = jnp.where(valid, grad, 0.0)
            weights[k, whole, :] = (grad * key_scale[k]).astype(jnp.bfloat16)
            if k == 0:
                weights[WIN + 1, whole, :] = (grad * row_scale).astype(jnp.bfloat16)
            else:
                rw_out[k - 1, here, :] = (grad * row_scale).astype(jnp.bfloat16)

    def dispatch(k):
        return copy(rw_out.at[k - 1], rw_in.at[k - 1, rows_of(m)], d_ss.at[k - 1], d_rs.at[k - 1], at_dp(k))

    for k in (2, 3, 1):
        dispatch(k).start()

    class Gather:
        def __init__(self, part, ss, rs):
            self.part, self.ss, self.rs = part, ss, rs
            known = [0]
            self.steps = []
            for bit in reversed(mp_bits):
                self.steps += [(s, bit) for s in known]
                known = known + [s ^ bit for s in known]
            self.steps.sort(key=lambda t: t[0])
            self.got = set()

        def hop(self, s, bit):
            part = self.part(s)
            return copy(part, part, self.ss.at[s ^ bit], self.rs.at[s ^ bit], (d, flip(m, bit)))

        def take(self, s):
            if s and s not in self.got:
                self.got.add(s)
                part = self.part(s)
                copy(part, part, self.ss.at[s], self.rs.at[s], (d, flip(m, 1))).wait_recv()

        def begin(self):
            for s, bit in self.steps:
                if s == 0:
                    self.hop(s, bit).start()

        def rest(self):
            for s, bit in self.steps:
                if s:
                    self.take(s)
                    self.hop(s, bit).start()

        def all(self):
            for s in range(1, nmp):
                self.take(s)

        def finish(self):
            for s, bit in self.steps:
                self.hop(s, bit).wait_send()

    local = Gather(lambda s: weights.at[:, across(s)], k_ss, k_rs)
    foreign = {k: Gather(lambda s, k=k: rw_in.at[k - 1, across(s)], g_ss.at[k - 1], g_rs.at[k - 1])
               for k in range(1, WIN + 1)}
    stages = []
    for bits, peer in ((mp_bits, lambda o: (d, flip_all(m, o))), (dp_bits, lambda o: (flip_all(d, o), m))):
        for i in range(0, len(bits), 2):
            pair = bits[i:i + 2]
            stages.append([peer(sum(pair[:1]))] if len(pair) == 1 else [peer(o) for o in (*pair, sum(pair))])

    def loss_copies(i):
        return [copy(lsum.at[i], lin.at[i, j], l_ss.at[i, j], l_rs.at[i, j], dev) for j, dev in enumerate(stages[i])]

    def loss_step(i):
        if i:
            for j, c in enumerate(loss_copies(i - 1)):
                c.wait_recv()
            lsum[i] = functools.reduce(lambda x, y: x + y, [lin[i - 1, j] for j in range(len(stages[i - 1]))], lsum[i - 1])
        if i < len(stages):
            for c in loss_copies(i):
                c.start()

    local.begin()
    loss_step(0)

    def back(w, x):
        return lax.dot_general(w, x, COLS_BY_ROWS, preferred_element_type=jnp.float32)

    far = 1 - parity
    mid = (1 + far, half_of(1 - far))
    late = (2 - far, half_of(far))

    def grad_query(r):
        at = rows_of(r)
        out = jnp.dot(weights[0, at, :], p_ref[...], preferred_element_type=jnp.float32)
        for k in range(WIN):
            out = out + jnp.dot(weights[k + 1, at, :], pbuf[k], preferred_element_type=jnp.float32)
        gq_ref[at, :] = out.astype(jnp.bfloat16)

    def grad_passage(terms, start, end):
        for r in range(2):
            at = pl.ds(r * half, half)
            out = [back(w[:, at], x) for w, x in terms()]
            out = functools.reduce(lambda x, y: x + y, out)
            if not start:
                out = acc[at, :] + out
            if end:
                gp_ref[at, :] = out.astype(jnp.bfloat16)
            else:
                acc[at, :] = out

    def piece(slot, at):
        return rw_in.at[slot, at], qbuf[slot, at, :]

    def foreign_begin(k):
        dispatch(k).wait_recv()
        foreign[k].begin()

    for c in range(2, CHUNKS):
        qs.relay(c)
        if c == middle:
            loss_step(1)
    for k in (2, 1, 3):
        foreign_begin(k)
    local.rest()
    qs.relay_late(first)
    local.all()
    for r in range(nmp):
        grad_query(r)
        if r == 1:
            qs.relay_late(first + 1)
    for c in range(first + 2, CHUNKS):
        qs.relay_late(c)
    grad_passage(lambda: [(weights.at[WIN + 1], q_ref[...])], True, False)
    for i in range(2, len(stages)):
        loss_step(i)
    for k in (2, 1, 3):
        foreign[k].rest()
    for k in (2, 1, 3):
        foreign[k].all()
    qs.early()
    grad_passage(lambda: [piece(0, half_of(0)), piece(0, half_of(1)), piece(1, half_of(0)), piece(*mid)], False, False)
    qs.late()
    grad_passage(lambda: [piece(*late)], False, False)
    loss_step(len(stages))
    total_count = functools.reduce(lambda x, y: x + y, [counts_ref[i] for i in range(ndp)])
    loss_ref[...] = lsum[len(stages), 0:1, 0:1] / total_count.astype(jnp.float32)
    qs.last()
    grad_passage(lambda: [piece(2, half_of(1))], False, True)

    ps.finish()
    qs.finish()
    for k in range(1, WIN + 1):
        dispatch(k).wait_send()
    for k in range(WIN + 1):
        for h in range(2):
            for j in range(1, nmp):
                tile_copy(k, h, j).wait_send()
    local.finish()
    for k in range(1, WIN + 1):
        foreign[k].finish()
    for i in range(len(stages)):
        for c in loss_copies(i):
            c.wait_send()


def local(ndp, nmp, query, passage, query_scale, passage_scale, partners, counts):
    rows, width = query.shape
    inv = 1.0 / math.sqrt(width * nmp)
    share = rows // nmp
    nst = sum(n.bit_length() // 2 for n in (ndp, nmp))
    bf, f32 = jnp.bfloat16, jnp.float32
    dma = pltpu.SemaphoreType.DMA
    vm = pl.BlockSpec(memory_space=pltpu.VMEM)
    hbm = pl.BlockSpec(memory_space=pltpu.HBM)
    gq, gp, loss = pl.pallas_call(
        functools.partial(kernel, ndp, nmp, inv),
        out_shape=[
            jax.ShapeDtypeStruct((rows, width), bf),
            jax.ShapeDtypeStruct((rows, width), bf),
            jax.ShapeDtypeStruct((1, 1), f32),
        ],
        in_specs=[hbm] * 6,
        out_specs=[vm] * 3,
        scratch_shapes=[
            pltpu.VMEM((rows, width), bf),
            pltpu.VMEM((rows, width), bf),
            pltpu.VMEM((rows,), bf),
            pltpu.VMEM((rows,), bf),
            pltpu.SMEM(partners.shape, jnp.int32),
            pltpu.SMEM(counts.shape, jnp.int32),
            pltpu.VMEM((WIN, rows, width), bf),
            pltpu.VMEM((WIN, rows, width), bf),
            pltpu.VMEM((8, rows), f32),
            pltpu.VMEM((WIN, 8, rows), f32),
            pltpu.VMEM((WIN + 1, 2, rows, rows // 2), f32),
            pltpu.VMEM((nmp - 1, WIN + 1, 2, share, rows // 2), f32),
            pltpu.VMEM((WIN + 2, rows, rows), bf),
            pltpu.VMEM((WIN, share, rows), bf),
            pltpu.VMEM((WIN, rows, rows), bf),
            pltpu.VMEM((rows, width), f32),
            pltpu.VMEM((nst + 1, 8, 128), f32),
            pltpu.VMEM((nst, 3, 8, 128), f32),
            dma((6,)),
            dma((4, CHUNKS + 1)), dma((WIN, CHUNKS + 1)),
            dma((4, CHUNKS + 1)), dma((WIN, CHUNKS + 1)),
            dma((nmp - 1, WIN + 1, 2)), dma((nmp - 1, WIN + 1, 2)),
            dma((nmp,)), dma((nmp,)),
            dma((WIN,)), dma((WIN,)),
            dma((WIN, nmp)), dma((WIN, nmp)),
            dma((nst, 3)), dma((nst, 3)),
        ],
        compiler_params=pltpu.CompilerParams(
            collective_id=0, has_side_effects=True, vmem_limit_bytes=48 * 1024 * 1024),
    )(*[pltpu.with_memory_space_constraint(x, pltpu.HBM)
        for x in (query, passage, passage_scale, query_scale, partners, counts)])
    return loss.reshape(()), gq, gp


def solution(mesh):
    return jax.shard_map(
        functools.partial(local, mesh.shape["dp"], mesh.shape["mp"]),
        mesh=mesh,
        in_specs=(P("dp", "mp"), P("dp", "mp"), P("dp"), P("dp"), P("dp", None), P()),
        out_specs=(P(), P("dp", "mp"), P("dp", "mp")),
        check_vma=False,
    )
```

```python
import functools
import math

import jax
import jax.numpy as jnp
from jax import lax
from jax.experimental import pallas as pl
from jax.experimental.pallas import tpu as pltpu
from jax.sharding import PartitionSpec as P

WIN = 3
CHUNKS = 8
FIRST = 5
FIRST_Q = 6
AHEAD = 6
GROUP = 32
MESH = pl.DeviceIdType.MESH
ROWS_BY_ROWS = (((1,), (1,)), ((), ()))
COLS_BY_ROWS = (((0,), (0,)), ((), ()))


def kernel(ndp, nmp, inv, q_hbm, p_hbm, ps_hbm, qs_hbm, partners_hbm, counts_hbm,
           gq_ref, gp_ref, loss_ref,
           q_ref, p_ref, ps_ref, qs_ref, partners_ref, counts_ref, pbuf, qbuf, psown, psbuf, raw, inbox, weights, rw_out, rw_in, acc, lsum, lin,
           own_sem, p_ss, p_rs, q_ss, q_rs, t_ss, t_rs, k_ss, k_rs,
           d_ss, d_rs, g_ss, g_rs, l_ss, l_rs):
    d = lax.axis_index("dp")
    m = lax.axis_index("mp")
    rows, width = q_ref.shape
    share = rows // nmp
    step = rows // CHUNKS
    half = rows // 2
    first = FIRST
    middle = CHUNKS // 2

    def at_dp(delta):
        return (lax.rem(d + delta + ndp, ndp), m)

    def flip(index, bit):
        return index + bit - 2 * bit * lax.rem(index // bit, 2)

    def flip_all(index, bits):
        for b in (1 << i for i in range(bits.bit_length())):
            if bits & b:
                index = flip(index, b)
        return index

    def rows_of(block):
        return pl.ds(pl.multiple_of(block * share, share), share)

    def half_of(h):
        return pl.ds(pl.multiple_of(h * half, half), half)

    even = lax.rem(d, 2) == 0
    odd = lax.rem(d, 2) == 1
    parity = lax.rem(d, 2)
    partner = (flip(d, 1), m)
    mp_bits = [1 << b for b in range(nmp.bit_length() - 1)]
    dp_bits = [1 << b for b in range(ndp.bit_length() - 1)]

    small = [(ps_hbm, ps_ref), (qs_hbm, qs_ref), (partners_hbm, partners_ref), (counts_hbm, counts_ref)]
    small = [pltpu.make_async_copy(src, dst, own_sem.at[2 + i]) for i, (src, dst) in enumerate(small)]
    own_q = pltpu.make_async_copy(q_hbm, q_ref, own_sem.at[0])
    own_p = pltpu.make_async_copy(p_hbm, p_ref, own_sem.at[1])

    peers = [partner, at_dp(2), at_dp(-2)]
    peers += [(d, flip(m, b)) for b in mp_bits]
    peers += [(flip(d, b), m) for b in dp_bits if b > WIN + 1]
    barrier = pltpu.get_barrier_semaphore()
    for peer in peers:
        pl.semaphore_signal(barrier, inc=1, device_id=peer, device_id_type=MESH)
    for c in small:
        c.start()
    own_q.start()
    own_p.start()
    small[0].wait()
    psown[...] = jnp.broadcast_to(ps_ref[...].astype(jnp.float32)[None, :], psown.shape)
    pl.semaphore_wait(barrier, len(peers))

    def copy(src, dst, ssem, rsem, dev):
        return pltpu.make_async_remote_copy(
            src_ref=src, dst_ref=dst, send_sem=ssem, recv_sem=rsem,
            device_id=dev, device_id_type=MESH)

    class Stream:
        def __init__(self, own, buf, ss, rs, dest, far, first, extra=None):
            self.own, self.buf, self.ss, self.rs, self.dest = own, buf, ss, rs, dest
            self.far, self.near, self.extra, self.first = far, jnp.logical_not(far), extra, first
            self.order = ([] if extra is None else [-1]) + list(range(CHUNKS))

        def cut(self, slot, c):
            own, buf = (self.own, self.buf) if c >= 0 else self.extra
            at = pl.ds(max(c, 0) * step, step if c >= 0 else own.shape[0])
            return own.at[at] if slot is None else buf.at[slot, at]

        def move(self, kind, source, target, c, dev):
            return copy(self.cut(source, c), self.cut(target, c),
                        self.ss.at[kind, c % (CHUNKS + 1)], self.rs.at[target, c % (CHUNKS + 1)], dev)

        def direct(self, c):
            return self.move(0, None, 1, c, self.dest)

        def across_own(self, c):
            return self.move(1, None, 0, c, partner)

        def across_one(self, c):
            return self.move(1, 1, 0, c, partner)

        def onward(self, c):
            return self.move(2, 0, 2, c, self.dest)

        def across_first(self, c):
            return self.move(3, 1, 2, c, partner)

        def across_second(self, c):
            return self.move(3, 2, 1, c, partner)

        def arrived(self, slot, c):
            self.move(0, slot, slot, c, partner).wait_recv()

        def begin_direct(self, far, order):
            @pl.when(self.far if far else self.near)
            def _():
                for c in order:
                    if c < self.first or not far:
                        self.direct(c).start()

        def begin_across(self, order):
            @pl.when(self.far)
            def _():
                for c in order:
                    self.across_own(c).start()

        def begin(self, order):
            @pl.when(self.far)
            def _():
                for c in order:
                    self.across_own(c).start()
                    if c < self.first:
                        self.direct(c).start()

            @pl.when(self.near)
            def _():
                for c in order:
                    self.direct(c).start()

        def relay(self, c):
            @pl.when(self.far)
            def _():
                if c < self.first:
                    self.arrived(1, c)
                    self.across_first(c).start()
                self.arrived(0, c)
                self.onward(c).start()

            @pl.when(self.near)
            def _():
                self.arrived(1, c)
                self.across_one(c).start()
                self.arrived(0, c)
                if c >= self.first:
                    self.onward(c).start()

        def early(self):
            @pl.when(self.far)
            def _():
                for c in range(middle):
                    self.arrived(2, c)

        def relay_late(self, c):
            @pl.when(self.far)
            def _():
                self.arrived(1, c)

            @pl.when(self.near)
            def _():
                self.arrived(2, c)
                self.across_second(c).start()

        def late(self):
            @pl.when(self.near)
            def _():
                for c in range(min(middle, self.first)):
                    self.arrived(2, c)

        def last(self):
            @pl.when(self.far)
            def _():
                for c in range(middle, CHUNKS):
                    self.arrived(2, c)

            @pl.when(self.near)
            def _():
                for c in range(middle, self.first):
                    self.arrived(2, c)

        def last_extra(self):
            self.arrived(2, -1)

        def finish(self):
            @pl.when(self.far)
            def _():
                for c in self.order:
                    self.across_own(c).wait_send()
                    self.onward(c).wait_send()
                    if c < self.first:
                        self.direct(c).wait_send()
                        self.across_first(c).wait_send()

            @pl.when(self.near)
            def _():
                for c in self.order:
                    self.direct(c).wait_send()
                    self.across_one(c).wait_send()
                    if c >= self.first:
                        self.onward(c).wait_send()
                        self.across_second(c).wait_send()

    ps = Stream(p_hbm, pbuf, p_ss, p_rs, at_dp(-2), odd, FIRST, (psown, psbuf))
    qs = Stream(q_hbm, qbuf, q_ss, q_rs, at_dp(2), even, FIRST_Q)

    ps.begin(ps.order)
    qs.begin_across(range(2))

    def across(s):
        block = m
        for b in mp_bits:
            if s & b:
                block = flip(block, b)
        return rows_of(block)

    def tile_copy(k, h, s):
        return copy(raw.at[k, h, across(s)], inbox.at[s - 1, k, h],
                    t_ss.at[s - 1, k, h], t_rs.at[s - 1, k, h], (d, flip(m, s & -s)))

    def tile_next(k, h):
        for bit in mp_bits[1:]:
            for s in range(bit, nmp, 2 * bit):
                for b in mp_bits:
                    if b < bit:
                        tile_copy(k, h, s | b).wait_recv()
                        raw[k, h, across(s), :] += inbox[(s | b) - 1, k, h]
                tile_copy(k, h, s).start()

    def tile(k, h, keys):
        raw[k, h] = lax.dot_general(q_ref[...], keys, ROWS_BY_ROWS, preferred_element_type=jnp.float32)
        for s in range(1, nmp, 2):
            tile_copy(k, h, s).start()

    def tile_far(k, h):
        tile(k, h, pbuf[k - 1, half_of(h), :])

    own_q.wait()
    own_p.wait()
    for h in range(2):
        tile(0, h, p_ref[h * half:(h + 1) * half, :])
    ps.relay(-1)
    ps.relay(0)
    for h in range(2):
        tile_next(0, h)
    for c in range(1, middle):
        ps.relay(c)
    tile_far(2, 0)
    ps.relay(middle)
    tile_next(2, 0)
    tile_far(1, 0)
    ps.relay(middle + 1)
    tile_next(1, 0)
    for c in range(middle + 2, CHUNKS):
        ps.relay(c)
    qs.begin_direct(True, range(FIRST_Q))
    tile_far(1, 1)
    ps.early()
    tile_far(2 + parity, 1 - parity)
    tile_next(1, 1)
    tile_next(2 + parity, 1 - parity)
    for c in range(first, CHUNKS):
        ps.relay_late(c)
        if c == first: qs.begin_direct(False, range(0, 2))
    qs.begin_across(range(2, CHUNKS))
    qs.begin_direct(False, range(2, AHEAD))
    ps.late()
    tile_far(3 - parity, parity)
    ps.last()
    tile_far(3, 1)
    tile_next(3 - parity, parity)
    tile_next(3, 1)
    ps.last_extra()
    for c in range(2):
        qs.relay(c)
    for c in small[1:]:
        c.wait()
    for k in range(WIN + 1):
        for h in range(2):
            for b in mp_bits:
                tile_copy(k, h, b).wait_recv()

    lsum[...] = jnp.zeros_like(lsum)
    live = [None] + [functools.reduce(jnp.logical_or, [partners_ref[0, j] == k for j in range(partners_ref.shape[1])])
                     for k in range(1, WIN + 1)]
    counted = [counts_ref[lax.rem(d + k, ndp)] for k in range(WIN + 1)]
    key_count = [counted[0]] + [jnp.where(live[k], counted[k], 0) for k in range(1, WIN + 1)]
    query_scale = qs_ref[...].astype(jnp.float32)[None, :]

    @pl.loop(0, share // GROUP)
    def _(g):
        low = pl.multiple_of(g * GROUP, GROUP)
        here = pl.ds(low, GROUP)
        whole = pl.ds(pl.multiple_of(m * share + low, GROUP), GROUP)
        cols = lax.broadcasted_iota(jnp.int32, (GROUP, rows), 1)
        ids = lax.broadcasted_iota(jnp.int32, (GROUP, rows), 0) + (m * share + low)
        diagonal = cols == ids
        row_scale = jnp.sum(jnp.where(diagonal, query_scale, 0.0), axis=1, keepdims=True)
        valid = ids[:, 0:1] < key_count[0]
        key_scale = [psown[0:1, :]] + [psbuf[k, 0:1, :] for k in range(WIN)]
        scores = []
        for k in range(WIN + 1):
            parts = []
            for h in range(2):
                s = raw[k, h, whole, :]
                for b in mp_bits:
                    s = s + inbox[b - 1, k, h, here, :]
                parts.append(s)
            scores.append(jnp.concatenate(parts, axis=1) * (row_scale * inv) * key_scale[k])
        masked = [jnp.where(cols < key_count[k], scores[k], -jnp.inf) for k in range(WIN + 1)]
        top = functools.reduce(jnp.maximum, [jnp.max(x, axis=1, keepdims=True) for x in masked])
        exps = [jnp.exp(x - top) for x in masked]
        total = sum(jnp.sum(x, axis=1, keepdims=True) for x in exps)
        lse = top + jnp.log(total)
        positive = jnp.sum(jnp.where(diagonal, scores[0], 0.0), axis=1, keepdims=True)
        lost = jnp.sum(jnp.where(valid, lse - positive, 0.0), axis=0, keepdims=True)
        lsum[0] = lsum[0] + lost
        for k in range(WIN + 1):
            grad = exps[k] / total
            if k == 0:
                grad = grad - diagonal.astype(jnp.float32)
            grad = jnp.where(valid, grad, 0.0)
            weights[k, whole, :] = (grad * key_scale[k]).astype(jnp.bfloat16)
            if k == 0:
                weights[WIN + 1, whole, :] = (grad * row_scale).astype(jnp.bfloat16)
            else:
                rw_out[k - 1, here, :] = (grad * row_scale).astype(jnp.bfloat16)

    def dispatch(k):
        return copy(rw_out.at[k - 1], rw_in.at[k - 1, rows_of(m)], d_ss.at[k - 1], d_rs.at[k - 1], at_dp(k))

    for k in (2, 3, 1):
        dispatch(k).start()

    class Gather:
        def __init__(self, part, ss, rs):
            self.part, self.ss, self.rs = part, ss, rs
            known = [0]
            self.steps = []
            for bit in reversed(mp_bits):
                self.steps += [(s, bit) for s in known]
                known = known + [s ^ bit for s in known]
            self.steps.sort(key=lambda t: t[0])
            self.got = set()

        def hop(self, s, bit):
            part = self.part(s)
            return copy(part, part, self.ss.at[s ^ bit], self.rs.at[s ^ bit], (d, flip(m, bit)))

        def take(self, s):
            if s and s not in self.got:
                self.got.add(s)
                part = self.part(s)
                copy(part, part, self.ss.at[s], self.rs.at[s], (d, flip(m, 1))).wait_recv()

        def begin(self):
            for s, bit in self.steps:
                if s == 0:
                    self.hop(s, bit).start()

        def rest(self):
            for s, bit in self.steps:
                if s:
                    self.take(s)
                    self.hop(s, bit).start()

        def all(self):
            for s in range(1, nmp):
                self.take(s)

        def finish(self):
            for s, bit in self.steps:
                self.hop(s, bit).wait_send()

    local = Gather(lambda s: weights.at[0:WIN + 1, across(s)], k_ss.at[0], k_rs.at[0])
    local_rows = Gather(lambda s: weights.at[WIN + 1, across(s)], k_ss.at[1], k_rs.at[1])
    foreign = {k: Gather(lambda s, k=k: rw_in.at[k - 1, across(s)], g_ss.at[k - 1], g_rs.at[k - 1])
               for k in range(1, WIN + 1)}
    stages = []
    for bits, peer in ((mp_bits, lambda o: (d, flip_all(m, o))), (dp_bits, lambda o: (flip_all(d, o), m))):
        for i in range(0, len(bits), 2):
            pair = bits[i:i + 2]
            stages.append([peer(sum(pair[:1]))] if len(pair) == 1 else [peer(o) for o in (*pair, sum(pair))])

    def loss_copies(i):
        return [copy(lsum.at[i], lin.at[i, j], l_ss.at[i, j], l_rs.at[i, j], dev) for j, dev in enumerate(stages[i])]

    def loss_step(i):
        if i:
            for j, c in enumerate(loss_copies(i - 1)):
                c.wait_recv()
            lsum[i] = functools.reduce(lambda x, y: x + y, [lin[i - 1, j] for j in range(len(stages[i - 1]))], lsum[i - 1])
        if i < len(stages):
            for c in loss_copies(i):
                c.start()

    qs.begin_direct(False, range(AHEAD, CHUNKS))
    local.begin()
    local_rows.begin()
    loss_step(0)

    def back(w, x):
        return lax.dot_general(w, x, COLS_BY_ROWS, preferred_element_type=jnp.float32)

    far = 1 - parity
    mid = (1 + far, half_of(1 - far))
    late = (2 - far, half_of(far))

    def grad_query(r):
        at = rows_of(r)
        out = jnp.dot(weights[0, at, :], p_ref[...], preferred_element_type=jnp.float32)
        for k in range(WIN):
            out = out + jnp.dot(weights[k + 1, at, :], pbuf[k], preferred_element_type=jnp.float32)
        gq_ref[at, :] = out.astype(jnp.bfloat16)

    def grad_passage(terms, start, end):
        for r in range(2):
            at = pl.ds(r * half, half)
            out = [back(w[:, at], x) for w, x in terms()]
            out = functools.reduce(lambda x, y: x + y, out)
            if not start:
                out = acc[at, :] + out
            if end:
                gp_ref[at, :] = out.astype(jnp.bfloat16)
            else:
                acc[at, :] = out

    def piece(slot, at):
        return rw_in.at[slot, at], qbuf[slot, at, :]

    def foreign_begin(k):
        dispatch(k).wait_recv()
        foreign[k].begin()

    for c in range(2, CHUNKS):
        qs.relay(c)
        if c == middle:
            loss_step(1)
    for k in (2, 1, 3):
        foreign_begin(k)
    local.rest()
    if FIRST_Q <= first:
        qs.relay_late(first)
    local.all()
    local_rows.rest()
    for r in range(nmp):
        grad_query(r)
        if r == 1:
            if FIRST_Q <= first + 1:
                qs.relay_late(first + 1)
    for c in range(max(FIRST_Q, first + 2), CHUNKS):
        qs.relay_late(c)
    local_rows.all()
    grad_passage(lambda: [(weights.at[WIN + 1], q_ref[...])], True, False)
    for i in range(2, len(stages)):
        loss_step(i)
    for k in (2, 1, 3):
        foreign[k].rest()
    for k in (2, 1, 3):
        foreign[k].all()
    qs.early()
    grad_passage(lambda: [piece(0, half_of(0)), piece(0, half_of(1)), piece(1, half_of(0)), piece(*mid)], False, False)
    qs.late()
    grad_passage(lambda: [piece(*late)], False, False)
    loss_step(len(stages))
    total_count = functools.reduce(lambda x, y: x + y, [counts_ref[i] for i in range(ndp)])
    loss_ref[...] = lsum[len(stages), 0:1, 0:1] / total_count.astype(jnp.float32)
    qs.last()
    grad_passage(lambda: [piece(2, half_of(1))], False, True)

    ps.finish()
    qs.finish()
    for k in range(1, WIN + 1):
        dispatch(k).wait_send()
    for k in range(WIN + 1):
        for h in range(2):
            for j in range(1, nmp):
                tile_copy(k, h, j).wait_send()
    local.finish()
    local_rows.finish()
    for k in range(1, WIN + 1):
        foreign[k].finish()
    for i in range(len(stages)):
        for c in loss_copies(i):
            c.wait_send()


def local(ndp, nmp, query, passage, query_scale, passage_scale, partners, counts):
    rows, width = query.shape
    inv = 1.0 / math.sqrt(width * nmp)
    share = rows // nmp
    nst = sum(n.bit_length() // 2 for n in (ndp, nmp))
    bf, f32 = jnp.bfloat16, jnp.float32
    dma = pltpu.SemaphoreType.DMA
    vm = pl.BlockSpec(memory_space=pltpu.VMEM)
    hbm = pl.BlockSpec(memory_space=pltpu.HBM)
    gq, gp, loss = pl.pallas_call(
        functools.partial(kernel, ndp, nmp, inv),
        out_shape=[
            jax.ShapeDtypeStruct((rows, width), bf),
            jax.ShapeDtypeStruct((rows, width), bf),
            jax.ShapeDtypeStruct((1, 1), f32),
        ],
        in_specs=[hbm] * 6,
        out_specs=[vm] * 3,
        scratch_shapes=[
            pltpu.VMEM((rows, width), bf),
            pltpu.VMEM((rows, width), bf),
            pltpu.VMEM((rows,), bf),
            pltpu.VMEM((rows,), bf),
            pltpu.SMEM(partners.shape, jnp.int32),
            pltpu.SMEM(counts.shape, jnp.int32),
            pltpu.VMEM((WIN, rows, width), bf),
            pltpu.VMEM((WIN, rows, width), bf),
            pltpu.VMEM((8, rows), f32),
            pltpu.VMEM((WIN, 8, rows), f32),
            pltpu.VMEM((WIN + 1, 2, rows, rows // 2), f32),
            pltpu.VMEM((nmp - 1, WIN + 1, 2, share, rows // 2), f32),
            pltpu.VMEM((WIN + 2, rows, rows), bf),
            pltpu.VMEM((WIN, share, rows), bf),
            pltpu.VMEM((WIN, rows, rows), bf),
            pltpu.VMEM((rows, width), f32),
            pltpu.VMEM((nst + 1, 8, 128), f32),
            pltpu.VMEM((nst, 3, 8, 128), f32),
            dma((6,)),
            dma((4, CHUNKS + 1)), dma((WIN, CHUNKS + 1)),
            dma((4, CHUNKS + 1)), dma((WIN, CHUNKS + 1)),
            dma((nmp - 1, WIN + 1, 2)), dma((nmp - 1, WIN + 1, 2)),
            dma((2, nmp)), dma((2, nmp)),
            dma((WIN,)), dma((WIN,)),
            dma((WIN, nmp)), dma((WIN, nmp)),
            dma((nst, 3)), dma((nst, 3)),
        ],
        compiler_params=pltpu.CompilerParams(
            collective_id=0, has_side_effects=True, vmem_limit_bytes=48 * 1024 * 1024),
    )(*[pltpu.with_memory_space_constraint(x, pltpu.HBM)
        for x in (query, passage, passage_scale, query_scale, partners, counts)])
    return loss.reshape(()), gq, gp


def solution(mesh):
    return jax.shard_map(
        functools.partial(local, mesh.shape["dp"], mesh.shape["mp"]),
        mesh=mesh,
        in_specs=(P("dp", "mp"), P("dp", "mp"), P("dp"), P("dp"), P("dp", None), P()),
        out_specs=(P(), P("dp", "mp"), P("dp", "mp")),
        check_vma=False,
    )
```

```python
import functools
import math

import jax
import jax.numpy as jnp
from jax import lax
from jax.experimental import pallas as pl
from jax.experimental.pallas import tpu as pltpu
from jax.sharding import PartitionSpec as P

WIN = 3
CHUNKS = 8
FIRST = 5
FIRST_Q = 6
AHEAD = 6
GROUP = 32
MESH = pl.DeviceIdType.MESH
ROWS_BY_ROWS = (((1,), (1,)), ((), ()))
COLS_BY_ROWS = (((0,), (0,)), ((), ()))


def kernel(ndp, nmp, inv, q_hbm, p_hbm, ps_hbm, qs_hbm, partners_hbm, counts_hbm,
           gq_ref, gp_ref, loss_ref,
           q_ref, p_ref, ps_ref, qs_ref, partners_ref, counts_ref, pbuf, qbuf, psown, psbuf, raw, inbox, weights, rw_out, rw_in, acc, lsum, lin,
           own_sem, p_ss, p_rs, q_ss, q_rs, t_ss, t_rs, k_ss, k_rs,
           d_ss, d_rs, g_ss, g_rs, l_ss, l_rs):
    d = lax.axis_index("dp")
    m = lax.axis_index("mp")
    rows, width = q_ref.shape
    share = rows // nmp
    step = rows // CHUNKS
    half = rows // 2
    first = FIRST
    middle = CHUNKS // 2

    def at_dp(delta):
        return (lax.rem(d + delta + ndp, ndp), m)

    def flip(index, bit):
        return index + bit - 2 * bit * lax.rem(index // bit, 2)

    def flip_all(index, bits):
        for b in (1 << i for i in range(bits.bit_length())):
            if bits & b:
                index = flip(index, b)
        return index

    def rows_of(block):
        return pl.ds(pl.multiple_of(block * share, share), share)

    def half_of(h):
        return pl.ds(pl.multiple_of(h * half, half), half)

    even = lax.rem(d, 2) == 0
    odd = lax.rem(d, 2) == 1
    parity = lax.rem(d, 2)
    partner = (flip(d, 1), m)
    mp_bits = [1 << b for b in range(nmp.bit_length() - 1)]
    dp_bits = [1 << b for b in range(ndp.bit_length() - 1)]

    small = [(ps_hbm, ps_ref), (qs_hbm, qs_ref), (partners_hbm, partners_ref), (counts_hbm, counts_ref)]
    small = [pltpu.make_async_copy(src, dst, own_sem.at[2 + i]) for i, (src, dst) in enumerate(small)]
    own_q = pltpu.make_async_copy(q_hbm, q_ref, own_sem.at[0])
    own_p = pltpu.make_async_copy(p_hbm, p_ref, own_sem.at[1])

    peers = [partner, at_dp(2), at_dp(-2)]
    peers += [(d, flip(m, b)) for b in mp_bits]
    peers += [(flip(d, b), m) for b in dp_bits if b > WIN + 1]
    barrier = pltpu.get_barrier_semaphore()
    for peer in peers:
        pl.semaphore_signal(barrier, inc=1, device_id=peer, device_id_type=MESH)
    for c in small:
        c.start()
    own_q.start()
    own_p.start()
    small[0].wait()
    psown[...] = jnp.broadcast_to(ps_ref[...].astype(jnp.float32)[None, :], psown.shape)
    pl.semaphore_wait(barrier, len(peers))

    def copy(src, dst, ssem, rsem, dev):
        return pltpu.make_async_remote_copy(
            src_ref=src, dst_ref=dst, send_sem=ssem, recv_sem=rsem,
            device_id=dev, device_id_type=MESH)

    class Stream:
        def __init__(self, own, buf, ss, rs, dest, far, first, extra=None):
            self.own, self.buf, self.ss, self.rs, self.dest = own, buf, ss, rs, dest
            self.far, self.near, self.extra, self.first = far, jnp.logical_not(far), extra, first
            self.order = ([] if extra is None else [-1]) + list(range(CHUNKS))

        def cut(self, slot, c):
            own, buf = (self.own, self.buf) if c >= 0 else self.extra
            at = pl.ds(max(c, 0) * step, step if c >= 0 else own.shape[0])
            return own.at[at] if slot is None else buf.at[slot, at]

        def move(self, kind, source, target, c, dev):
            return copy(self.cut(source, c), self.cut(target, c),
                        self.ss.at[kind, c % (CHUNKS + 1)], self.rs.at[target, c % (CHUNKS + 1)], dev)

        def direct(self, c):
            return self.move(0, None, 1, c, self.dest)

        def across_own(self, c):
            return self.move(1, None, 0, c, partner)

        def across_one(self, c):
            return self.move(1, 1, 0, c, partner)

        def onward(self, c):
            return self.move(2, 0, 2, c, self.dest)

        def across_first(self, c):
            return self.move(3, 1, 2, c, partner)

        def across_second(self, c):
            return self.move(3, 2, 1, c, partner)

        def arrived(self, slot, c):
            self.move(0, slot, slot, c, partner).wait_recv()

        def begin_direct(self, far, order):
            @pl.when(self.far if far else self.near)
            def _():
                for c in order:
                    if c < self.first or not far:
                        self.direct(c).start()

        def begin_across(self, order):
            @pl.when(self.far)
            def _():
                for c in order:
                    self.across_own(c).start()

        def begin(self, order):
            @pl.when(self.far)
            def _():
                for c in order:
                    self.across_own(c).start()
                    if c < self.first:
                        self.direct(c).start()

            @pl.when(self.near)
            def _():
                for c in order:
                    self.direct(c).start()

        def relay(self, c):
            @pl.when(self.far)
            def _():
                if c < self.first:
                    self.arrived(1, c)
                    self.across_first(c).start()
                self.arrived(0, c)
                self.onward(c).start()

            @pl.when(self.near)
            def _():
                self.arrived(1, c)
                self.across_one(c).start()
                self.arrived(0, c)
                if c >= self.first:
                    self.onward(c).start()

        def early(self):
            @pl.when(self.far)
            def _():
                for c in range(middle):
                    self.arrived(2, c)

        def relay_late(self, c):
            @pl.when(self.far)
            def _():
                self.arrived(1, c)

            @pl.when(self.near)
            def _():
                self.arrived(2, c)
                self.across_second(c).start()

        def late(self):
            @pl.when(self.near)
            def _():
                for c in range(min(middle, self.first)):
                    self.arrived(2, c)

        def last(self):
            @pl.when(self.far)
            def _():
                for c in range(middle, CHUNKS):
                    self.arrived(2, c)

            @pl.when(self.near)
            def _():
                for c in range(middle, self.first):
                    self.arrived(2, c)

        def last_extra(self):
            self.arrived(2, -1)

        def finish(self):
            @pl.when(self.far)
            def _():
                for c in self.order:
                    self.across_own(c).wait_send()
                    self.onward(c).wait_send()
                    if c < self.first:
                        self.direct(c).wait_send()
                        self.across_first(c).wait_send()

            @pl.when(self.near)
            def _():
                for c in self.order:
                    self.direct(c).wait_send()
                    self.across_one(c).wait_send()
                    if c >= self.first:
                        self.onward(c).wait_send()
                        self.across_second(c).wait_send()

    ps = Stream(p_hbm, pbuf, p_ss, p_rs, at_dp(-2), odd, FIRST, (psown, psbuf))
    qs = Stream(q_hbm, qbuf, q_ss, q_rs, at_dp(2), even, FIRST_Q)

    ps.begin(ps.order)
    qs.begin_across(range(2))

    def across(s):
        block = m
        for b in mp_bits:
            if s & b:
                block = flip(block, b)
        return rows_of(block)

    def tile_copy(k, h, s):
        return copy(raw.at[k, h, across(s)], inbox.at[s - 1, k, h],
                    t_ss.at[s - 1, k, h], t_rs.at[s - 1, k, h], (d, flip(m, s & -s)))

    def tile_next(k, h):
        for bit in mp_bits[1:]:
            for s in range(bit, nmp, 2 * bit):
                for b in mp_bits:
                    if b < bit:
                        tile_copy(k, h, s | b).wait_recv()
                        raw[k, h, across(s), :] += inbox[(s | b) - 1, k, h]
                tile_copy(k, h, s).start()

    def tile(k, h, keys):
        raw[k, h] = lax.dot_general(q_ref[...], keys, ROWS_BY_ROWS, preferred_element_type=jnp.float32)
        for s in range(1, nmp, 2):
            tile_copy(k, h, s).start()

    def tile_far(k, h):
        tile(k, h, pbuf[k - 1, half_of(h), :])

    own_q.wait()
    own_p.wait()
    for h in range(2):
        tile(0, h, p_ref[h * half:(h + 1) * half, :])
    ps.relay(-1)
    ps.relay(0)
    for h in range(2):
        tile_next(0, h)
    for c in range(1, middle):
        ps.relay(c)
    tile_far(2, 0)
    ps.relay(middle)
    tile_next(2, 0)
    tile_far(1, 0)
    ps.relay(middle + 1)
    tile_next(1, 0)
    for c in range(middle + 2, CHUNKS):
        ps.relay(c)
    qs.begin_direct(True, range(FIRST_Q))
    tile_far(1, 1)
    ps.early()
    tile_far(2 + parity, 1 - parity)
    tile_next(1, 1)
    tile_next(2 + parity, 1 - parity)
    for c in range(first, CHUNKS):
        ps.relay_late(c)
        if c == first: qs.begin_direct(False, range(0, 2))
    qs.begin_across(range(2, CHUNKS))
    qs.begin_direct(False, range(2, AHEAD))
    ps.late()
    tile_far(3 - parity, parity)
    ps.last()
    tile_far(3, 1)
    tile_next(3 - parity, parity)
    tile_next(3, 1)
    ps.last_extra()
    for c in range(2):
        qs.relay(c)
    for c in small[1:]:
        c.wait()
    for k in range(WIN + 1):
        for h in range(2):
            for b in mp_bits:
                tile_copy(k, h, b).wait_recv()

    lsum[...] = jnp.zeros_like(lsum)
    live = [None] + [functools.reduce(jnp.logical_or, [partners_ref[0, j] == k for j in range(partners_ref.shape[1])])
                     for k in range(1, WIN + 1)]
    counted = [counts_ref[lax.rem(d + k, ndp)] for k in range(WIN + 1)]
    key_count = [counted[0]] + [jnp.where(live[k], counted[k], 0) for k in range(1, WIN + 1)]
    query_scale = qs_ref[...].astype(jnp.float32)[None, :]

    @pl.loop(0, share // GROUP)
    def _(g):
        low = pl.multiple_of(g * GROUP, GROUP)
        here = pl.ds(low, GROUP)
        whole = pl.ds(pl.multiple_of(m * share + low, GROUP), GROUP)
        cols = lax.broadcasted_iota(jnp.int32, (GROUP, rows), 1)
        ids = lax.broadcasted_iota(jnp.int32, (GROUP, rows), 0) + (m * share + low)
        diagonal = cols == ids
        row_scale = jnp.sum(jnp.where(diagonal, query_scale, 0.0), axis=1, keepdims=True)
        valid = ids[:, 0:1] < key_count[0]
        key_scale = [psown[0:1, :]] + [psbuf[k, 0:1, :] for k in range(WIN)]
        scores = []
        for k in range(WIN + 1):
            parts = []
            for h in range(2):
                s = raw[k, h, whole, :]
                for b in mp_bits:
                    s = s + inbox[b - 1, k, h, here, :]
                parts.append(s)
            scores.append(jnp.concatenate(parts, axis=1) * (row_scale * inv) * key_scale[k])
        masked = [jnp.where(cols < key_count[k], scores[k], -jnp.inf) for k in range(WIN + 1)]
        top = functools.reduce(jnp.maximum, [jnp.max(x, axis=1, keepdims=True) for x in masked])
        exps = [jnp.exp(x - top) for x in masked]
        total = sum(jnp.sum(x, axis=1, keepdims=True) for x in exps)
        lse = top + jnp.log(total)
        positive = jnp.sum(jnp.where(diagonal, scores[0], 0.0), axis=1, keepdims=True)
        lost = jnp.sum(jnp.where(valid, lse - positive, 0.0), axis=0, keepdims=True)
        lsum[0] = lsum[0] + lost
        for k in range(WIN + 1):
            grad = exps[k] / total
            if k == 0:
                grad = grad - diagonal.astype(jnp.float32)
            grad = jnp.where(valid, grad, 0.0)
            weights[k, whole, :] = (grad * key_scale[k]).astype(jnp.bfloat16)
            if k == 0:
                weights[WIN + 1, whole, :] = (grad * row_scale).astype(jnp.bfloat16)
            else:
                rw_out[k - 1, here, :] = (grad * row_scale).astype(jnp.bfloat16)

    def dispatch(k):
        return copy(rw_out.at[k - 1], rw_in.at[k - 1, rows_of(m)], d_ss.at[k - 1], d_rs.at[k - 1], at_dp(k))

    for k in (2, 3, 1):
        dispatch(k).start()

    class Gather:
        def __init__(self, part, ss, rs):
            self.part, self.ss, self.rs = part, ss, rs
            known = [0]
            self.steps = []
            for bit in reversed(mp_bits):
                self.steps += [(s, bit) for s in known]
                known = known + [s ^ bit for s in known]
            self.steps.sort(key=lambda t: t[0])
            self.got = set()

        def hop(self, s, bit):
            part = self.part(s)
            return copy(part, part, self.ss.at[s ^ bit], self.rs.at[s ^ bit], (d, flip(m, bit)))

        def take(self, s):
            if s and s not in self.got:
                self.got.add(s)
                part = self.part(s)
                copy(part, part, self.ss.at[s], self.rs.at[s], (d, flip(m, 1))).wait_recv()

        def begin(self):
            for s, bit in self.steps:
                if s == 0:
                    self.hop(s, bit).start()

        def rest(self):
            for s, bit in self.steps:
                if s:
                    self.take(s)
                    self.hop(s, bit).start()

        def all(self):
            for s in range(1, nmp):
                self.take(s)

        def finish(self):
            for s, bit in self.steps:
                self.hop(s, bit).wait_send()

    local = Gather(lambda s: weights.at[0:WIN + 1, across(s)], k_ss.at[0], k_rs.at[0])
    local_rows = Gather(lambda s: weights.at[WIN + 1, across(s)], k_ss.at[1], k_rs.at[1])
    foreign = {k: Gather(lambda s, k=k: rw_in.at[k - 1, across(s)], g_ss.at[k - 1], g_rs.at[k - 1])
               for k in range(1, WIN + 1)}
    stages = []
    for bits, peer in ((mp_bits, lambda o: (d, flip_all(m, o))), (dp_bits, lambda o: (flip_all(d, o), m))):
        for i in range(0, len(bits), 2):
            pair = bits[i:i + 2]
            stages.append([peer(sum(pair[:1]))] if len(pair) == 1 else [peer(o) for o in (*pair, sum(pair))])

    def loss_copies(i):
        return [copy(lsum.at[i], lin.at[i, j], l_ss.at[i, j], l_rs.at[i, j], dev) for j, dev in enumerate(stages[i])]

    def loss_step(i):
        if i:
            for j, c in enumerate(loss_copies(i - 1)):
                c.wait_recv()
            lsum[i] = functools.reduce(lambda x, y: x + y, [lin[i - 1, j] for j in range(len(stages[i - 1]))], lsum[i - 1])
        if i < len(stages):
            for c in loss_copies(i):
                c.start()

    qs.begin_direct(False, range(AHEAD, CHUNKS))
    local.begin()
    local_rows.begin()
    loss_step(0)

    def back(w, x):
        return lax.dot_general(w, x, COLS_BY_ROWS, preferred_element_type=jnp.float32)

    far = 1 - parity
    mid = (1 + far, half_of(1 - far))
    late = (2 - far, half_of(far))

    def grad_query(r):
        at = rows_of(r)
        out = jnp.dot(weights[0, at, :], p_ref[...], preferred_element_type=jnp.float32)
        for k in range(WIN):
            out = out + jnp.dot(weights[k + 1, at, :], pbuf[k], preferred_element_type=jnp.float32)
        gq_ref[at, :] = out.astype(jnp.bfloat16)

    def grad_passage(terms, start, end):
        for r in range(2):
            at = pl.ds(r * half, half)
            out = [back(w[:, at], x) for w, x in terms()]
            out = functools.reduce(lambda x, y: x + y, out)
            if not start:
                out = acc[at, :] + out
            if end:
                gp_ref[at, :] = out.astype(jnp.bfloat16)
            else:
                acc[at, :] = out

    def piece(slot, at):
        return rw_in.at[slot, at], qbuf[slot, at, :]

    def foreign_begin(k):
        dispatch(k).wait_recv()
        foreign[k].begin()

    for c in range(2, CHUNKS):
        qs.relay(c)
        if c == middle:
            loss_step(1)
        if c == CHUNKS - 2:
            foreign_begin(2)
    for k in (1, 3):
        foreign_begin(k)
    local.rest()
    if FIRST_Q <= first:
        qs.relay_late(first)
    local.all()
    local_rows.rest()
    for r in range(nmp):
        grad_query(r)
        if r == 1:
            if FIRST_Q <= first + 1:
                qs.relay_late(first + 1)
    for c in range(max(FIRST_Q, first + 2), CHUNKS):
        qs.relay_late(c)
    local_rows.all()
    grad_passage(lambda: [(weights.at[WIN + 1], q_ref[...])], True, False)
    for i in range(2, len(stages)):
        loss_step(i)
    for k in (2, 1, 3):
        foreign[k].rest()
    for k in (2, 1, 3):
        foreign[k].all()
    qs.early()
    grad_passage(lambda: [piece(0, half_of(0)), piece(0, half_of(1)), piece(1, half_of(0)), piece(*mid)], False, False)
    qs.late()
    grad_passage(lambda: [piece(*late)], False, False)
    loss_step(len(stages))
    total_count = functools.reduce(lambda x, y: x + y, [counts_ref[i] for i in range(ndp)])
    loss_ref[...] = lsum[len(stages), 0:1, 0:1] / total_count.astype(jnp.float32)
    qs.last()
    grad_passage(lambda: [piece(2, half_of(1))], False, True)

    ps.finish()
    qs.finish()
    for k in range(1, WIN + 1):
        dispatch(k).wait_send()
    for k in range(WIN + 1):
        for h in range(2):
            for j in range(1, nmp):
                tile_copy(k, h, j).wait_send()
    local.finish()
    local_rows.finish()
    for k in range(1, WIN + 1):
        foreign[k].finish()
    for i in range(len(stages)):
        for c in loss_copies(i):
            c.wait_send()


def local(ndp, nmp, query, passage, query_scale, passage_scale, partners, counts):
    rows, width = query.shape
    inv = 1.0 / math.sqrt(width * nmp)
    share = rows // nmp
    nst = sum(n.bit_length() // 2 for n in (ndp, nmp))
    bf, f32 = jnp.bfloat16, jnp.float32
    dma = pltpu.SemaphoreType.DMA
    vm = pl.BlockSpec(memory_space=pltpu.VMEM)
    hbm = pl.BlockSpec(memory_space=pltpu.HBM)
    gq, gp, loss = pl.pallas_call(
        functools.partial(kernel, ndp, nmp, inv),
        out_shape=[
            jax.ShapeDtypeStruct((rows, width), bf),
            jax.ShapeDtypeStruct((rows, width), bf),
            jax.ShapeDtypeStruct((1, 1), f32),
        ],
        in_specs=[hbm] * 6,
        out_specs=[vm] * 3,
        scratch_shapes=[
            pltpu.VMEM((rows, width), bf),
            pltpu.VMEM((rows, width), bf),
            pltpu.VMEM((rows,), bf),
            pltpu.VMEM((rows,), bf),
            pltpu.SMEM(partners.shape, jnp.int32),
            pltpu.SMEM(counts.shape, jnp.int32),
            pltpu.VMEM((WIN, rows, width), bf),
            pltpu.VMEM((WIN, rows, width), bf),
            pltpu.VMEM((8, rows), f32),
            pltpu.VMEM((WIN, 8, rows), f32),
            pltpu.VMEM((WIN + 1, 2, rows, rows // 2), f32),
            pltpu.VMEM((nmp - 1, WIN + 1, 2, share, rows // 2), f32),
            pltpu.VMEM((WIN + 2, rows, rows), bf),
            pltpu.VMEM((WIN, share, rows), bf),
            pltpu.VMEM((WIN, rows, rows), bf),
            pltpu.VMEM((rows, width), f32),
            pltpu.VMEM((nst + 1, 8, 128), f32),
            pltpu.VMEM((nst, 3, 8, 128), f32),
            dma((6,)),
            dma((4, CHUNKS + 1)), dma((WIN, CHUNKS + 1)),
            dma((4, CHUNKS + 1)), dma((WIN, CHUNKS + 1)),
            dma((nmp - 1, WIN + 1, 2)), dma((nmp - 1, WIN + 1, 2)),
            dma((2, nmp)), dma((2, nmp)),
            dma((WIN,)), dma((WIN,)),
            dma((WIN, nmp)), dma((WIN, nmp)),
            dma((nst, 3)), dma((nst, 3)),
        ],
        compiler_params=pltpu.CompilerParams(
            collective_id=0, has_side_effects=True, vmem_limit_bytes=48 * 1024 * 1024),
    )(*[pltpu.with_memory_space_constraint(x, pltpu.HBM)
        for x in (query, passage, passage_scale, query_scale, partners, counts)])
    return loss.reshape(()), gq, gp


def solution(mesh):
    return jax.shard_map(
        functools.partial(local, mesh.shape["dp"], mesh.shape["mp"]),
        mesh=mesh,
        in_specs=(P("dp", "mp"), P("dp", "mp"), P("dp"), P("dp"), P("dp", None), P()),
        out_specs=(P(), P("dp", "mp"), P("dp", "mp")),
        check_vma=False,
    )
```

```python
import functools
import math

import jax
import jax.numpy as jnp
from jax import lax
from jax.experimental import pallas as pl
from jax.experimental.pallas import tpu as pltpu
from jax.sharding import PartitionSpec as P

WIN = 3
CHUNKS = 8
FIRST = 5
FIRST_Q = 6
AHEAD = 6
GROUP = 32
MESH = pl.DeviceIdType.MESH
ROWS_BY_ROWS = (((1,), (1,)), ((), ()))
COLS_BY_ROWS = (((0,), (0,)), ((), ()))


def kernel(ndp, nmp, inv, q_hbm, p_hbm, ps_hbm, qs_hbm, partners_hbm, counts_hbm,
           gq_ref, gp_ref, loss_ref,
           q_ref, p_ref, ps_ref, qs_ref, partners_ref, counts_ref, pbuf, qbuf, psown, psbuf, raw, inbox, weights, rw_out, rw_in, acc, lsum, lin,
           own_sem, p_ss, p_rs, q_ss, q_rs, t_ss, t_rs, k_ss, k_rs,
           d_ss, d_rs, g_ss, g_rs, l_ss, l_rs):
    d = lax.axis_index("dp")
    m = lax.axis_index("mp")
    rows, width = q_ref.shape
    share = rows // nmp
    step = rows // CHUNKS
    half = rows // 2
    first = FIRST
    middle = CHUNKS // 2

    def at_dp(delta):
        return (lax.rem(d + delta + ndp, ndp), m)

    def flip(index, bit):
        return index + bit - 2 * bit * lax.rem(index // bit, 2)

    def flip_all(index, bits):
        for b in (1 << i for i in range(bits.bit_length())):
            if bits & b:
                index = flip(index, b)
        return index

    def rows_of(block):
        return pl.ds(pl.multiple_of(block * share, share), share)

    def half_of(h):
        return pl.ds(pl.multiple_of(h * half, half), half)

    even = lax.rem(d, 2) == 0
    odd = lax.rem(d, 2) == 1
    parity = lax.rem(d, 2)
    partner = (flip(d, 1), m)
    mp_bits = [1 << b for b in range(nmp.bit_length() - 1)]
    dp_bits = [1 << b for b in range(ndp.bit_length() - 1)]

    small = [(ps_hbm, ps_ref), (qs_hbm, qs_ref), (partners_hbm, partners_ref), (counts_hbm, counts_ref)]
    small = [pltpu.make_async_copy(src, dst, own_sem.at[2 + i]) for i, (src, dst) in enumerate(small)]
    own_q = pltpu.make_async_copy(q_hbm, q_ref, own_sem.at[0])
    own_p = pltpu.make_async_copy(p_hbm, p_ref, own_sem.at[1])

    peers = [partner, at_dp(2), at_dp(-2)]
    peers += [(d, flip(m, b)) for b in mp_bits]
    jumps = {sum(c) for i in range(0, len(dp_bits), 2) for c in (dp_bits[i:i + 1], dp_bits[i + 1:i + 2], dp_bits[i:i + 2])}
    peers += [(flip_all(d, o), m) for o in sorted(jumps) if o > WIN + 1]
    barrier = pltpu.get_barrier_semaphore()
    for peer in peers:
        pl.semaphore_signal(barrier, inc=1, device_id=peer, device_id_type=MESH)
    for c in small:
        c.start()
    own_q.start()
    own_p.start()
    small[0].wait()
    psown[...] = jnp.broadcast_to(ps_ref[...].astype(jnp.float32)[None, :], psown.shape)
    pl.semaphore_wait(barrier, len(peers))

    def copy(src, dst, ssem, rsem, dev):
        return pltpu.make_async_remote_copy(
            src_ref=src, dst_ref=dst, send_sem=ssem, recv_sem=rsem,
            device_id=dev, device_id_type=MESH)

    class Stream:
        def __init__(self, own, buf, ss, rs, dest, far, first, extra=None):
            self.own, self.buf, self.ss, self.rs, self.dest = own, buf, ss, rs, dest
            self.far, self.near, self.extra, self.first = far, jnp.logical_not(far), extra, first
            self.order = ([] if extra is None else [-1]) + list(range(CHUNKS))

        def cut(self, slot, c):
            own, buf = (self.own, self.buf) if c >= 0 else self.extra
            at = pl.ds(max(c, 0) * step, step if c >= 0 else own.shape[0])
            return own.at[at] if slot is None else buf.at[slot, at]

        def move(self, kind, source, target, c, dev):
            return copy(self.cut(source, c), self.cut(target, c),
                        self.ss.at[kind, c % (CHUNKS + 1)], self.rs.at[target, c % (CHUNKS + 1)], dev)

        def direct(self, c):
            return self.move(0, None, 1, c, self.dest)

        def across_own(self, c):
            return self.move(1, None, 0, c, partner)

        def across_one(self, c):
            return self.move(1, 1, 0, c, partner)

        def onward(self, c):
            return self.move(2, 0, 2, c, self.dest)

        def across_first(self, c):
            return self.move(3, 1, 2, c, partner)

        def across_second(self, c):
            return self.move(3, 2, 1, c, partner)

        def arrived(self, slot, c):
            self.move(0, slot, slot, c, partner).wait_recv()

        def begin_direct(self, far, order):
            @pl.when(self.far if far else self.near)
            def _():
                for c in order:
                    if c < self.first or not far:
                        self.direct(c).start()

        def begin_across(self, order):
            @pl.when(self.far)
            def _():
                for c in order:
                    self.across_own(c).start()

        def begin(self, order):
            @pl.when(self.far)
            def _():
                for c in order:
                    self.across_own(c).start()
                    if c < self.first:
                        self.direct(c).start()

            @pl.when(self.near)
            def _():
                for c in order:
                    self.direct(c).start()

        def relay(self, c):
            @pl.when(self.far)
            def _():
                if c < self.first:
                    self.arrived(1, c)
                    self.across_first(c).start()
                self.arrived(0, c)
                self.onward(c).start()

            @pl.when(self.near)
            def _():
                self.arrived(1, c)
                self.across_one(c).start()
                self.arrived(0, c)
                if c >= self.first:
                    self.onward(c).start()

        def early(self):
            @pl.when(self.far)
            def _():
                for c in range(middle):
                    self.arrived(2, c)

        def relay_late(self, c):
            @pl.when(self.far)
            def _():
                self.arrived(1, c)

            @pl.when(self.near)
            def _():
                self.arrived(2, c)
                self.across_second(c).start()

        def late(self):
            @pl.when(self.near)
            def _():
                for c in range(min(middle, self.first)):
                    self.arrived(2, c)

        def last(self):
            @pl.when(self.far)
            def _():
                for c in range(middle, CHUNKS):
                    self.arrived(2, c)

            @pl.when(self.near)
            def _():
                for c in range(middle, self.first):
                    self.arrived(2, c)

        def last_extra(self):
            self.arrived(2, -1)

        def finish(self):
            @pl.when(self.far)
            def _():
                for c in self.order:
                    self.across_own(c).wait_send()
                    self.onward(c).wait_send()
                    if c < self.first:
                        self.direct(c).wait_send()
                        self.across_first(c).wait_send()

            @pl.when(self.near)
            def _():
                for c in self.order:
                    self.direct(c).wait_send()
                    self.across_one(c).wait_send()
                    if c >= self.first:
                        self.onward(c).wait_send()
                        self.across_second(c).wait_send()

    ps = Stream(p_hbm, pbuf, p_ss, p_rs, at_dp(-2), odd, FIRST, (psown, psbuf))
    qs = Stream(q_hbm, qbuf, q_ss, q_rs, at_dp(2), even, FIRST_Q)

    ps.begin(ps.order)
    qs.begin_across(range(2))

    def across(s):
        block = m
        for b in mp_bits:
            if s & b:
                block = flip(block, b)
        return rows_of(block)

    def tile_copy(k, h, s):
        return copy(raw.at[k, h, across(s)], inbox.at[s - 1, k, h],
                    t_ss.at[s - 1, k, h], t_rs.at[s - 1, k, h], (d, flip(m, s & -s)))

    def tile_next(k, h):
        for bit in mp_bits[1:]:
            for s in range(bit, nmp, 2 * bit):
                for b in mp_bits:
                    if b < bit:
                        tile_copy(k, h, s | b).wait_recv()
                        raw[k, h, across(s), :] += inbox[(s | b) - 1, k, h]
                tile_copy(k, h, s).start()

    def tile(k, h, keys):
        raw[k, h] = lax.dot_general(q_ref[...], keys, ROWS_BY_ROWS, preferred_element_type=jnp.float32)
        for s in range(1, nmp, 2):
            tile_copy(k, h, s).start()

    def tile_far(k, h):
        tile(k, h, pbuf[k - 1, half_of(h), :])

    own_q.wait()
    own_p.wait()
    for h in range(2):
        tile(0, h, p_ref[h * half:(h + 1) * half, :])
    ps.relay(-1)
    ps.relay(0)
    for h in range(2):
        tile_next(0, h)
    for c in range(1, middle):
        ps.relay(c)
    tile_far(2, 0)
    ps.relay(middle)
    tile_next(2, 0)
    tile_far(1, 0)
    ps.relay(middle + 1)
    tile_next(1, 0)
    for c in range(middle + 2, CHUNKS):
        ps.relay(c)
    qs.begin_direct(True, range(FIRST_Q))
    tile_far(1, 1)
    ps.early()
    tile_far(2 + parity, 1 - parity)
    tile_next(1, 1)
    tile_next(2 + parity, 1 - parity)
    for c in range(first, CHUNKS):
        ps.relay_late(c)
        if c == first: qs.begin_direct(False, range(0, 2))
    qs.begin_across(range(2, CHUNKS))
    qs.begin_direct(False, range(2, AHEAD))
    ps.late()
    tile_far(3 - parity, parity)
    ps.last()
    tile_far(3, 1)
    tile_next(3 - parity, parity)
    tile_next(3, 1)
    ps.last_extra()
    for c in range(2):
        qs.relay(c)
    for c in small[1:]:
        c.wait()
    for k in range(WIN + 1):
        for h in range(2):
            for b in mp_bits:
                tile_copy(k, h, b).wait_recv()

    lsum[...] = jnp.zeros_like(lsum)
    live = [None] + [functools.reduce(jnp.logical_or, [partners_ref[0, j] == k for j in range(partners_ref.shape[1])])
                     for k in range(1, WIN + 1)]
    counted = [counts_ref[lax.rem(d + k, ndp)] for k in range(WIN + 1)]
    key_count = [counted[0]] + [jnp.where(live[k], counted[k], 0) for k in range(1, WIN + 1)]
    query_scale = qs_ref[...].astype(jnp.float32)[None, :]

    @pl.loop(0, share // GROUP)
    def _(g):
        low = pl.multiple_of(g * GROUP, GROUP)
        here = pl.ds(low, GROUP)
        whole = pl.ds(pl.multiple_of(m * share + low, GROUP), GROUP)
        cols = lax.broadcasted_iota(jnp.int32, (GROUP, rows), 1)
        ids = lax.broadcasted_iota(jnp.int32, (GROUP, rows), 0) + (m * share + low)
        diagonal = cols == ids
        row_scale = jnp.sum(jnp.where(diagonal, query_scale, 0.0), axis=1, keepdims=True)
        valid = ids[:, 0:1] < key_count[0]
        key_scale = [psown[0:1, :]] + [psbuf[k, 0:1, :] for k in range(WIN)]
        scores = []
        for k in range(WIN + 1):
            parts = []
            for h in range(2):
                s = raw[k, h, whole, :]
                for b in mp_bits:
                    s = s + inbox[b - 1, k, h, here, :]
                parts.append(s)
            scores.append(jnp.concatenate(parts, axis=1) * (row_scale * inv) * key_scale[k])
        masked = [jnp.where(cols < key_count[k], scores[k], -jnp.inf) for k in range(WIN + 1)]
        top = functools.reduce(jnp.maximum, [jnp.max(x, axis=1, keepdims=True) for x in masked])
        exps = [jnp.exp(x - top) for x in masked]
        total = sum(jnp.sum(x, axis=1, keepdims=True) for x in exps)
        lse = top + jnp.log(total)
        positive = jnp.sum(jnp.where(diagonal, scores[0], 0.0), axis=1, keepdims=True)
        lost = jnp.sum(jnp.where(valid, lse - positive, 0.0), axis=0, keepdims=True)
        lsum[0] = lsum[0] + lost
        for k in range(WIN + 1):
            grad = exps[k] / total
            if k == 0:
                grad = grad - diagonal.astype(jnp.float32)
            grad = jnp.where(valid, grad, 0.0)
            weights[k, whole, :] = (grad * key_scale[k]).astype(jnp.bfloat16)
            if k == 0:
                weights[WIN + 1, whole, :] = (grad * row_scale).astype(jnp.bfloat16)
            else:
                rw_out[k - 1, here, :] = (grad * row_scale).astype(jnp.bfloat16)

    def dispatch(k):
        return copy(rw_out.at[k - 1], rw_in.at[k - 1, rows_of(m)], d_ss.at[k - 1], d_rs.at[k - 1], at_dp(k))

    for k in (2, 3, 1):
        dispatch(k).start()

    class Gather:
        def __init__(self, part, ss, rs):
            self.part, self.ss, self.rs = part, ss, rs
            known = [0]
            self.steps = []
            for bit in reversed(mp_bits):
                self.steps += [(s, bit) for s in known]
                known = known + [s ^ bit for s in known]
            self.steps.sort(key=lambda t: t[0])
            self.got = set()

        def hop(self, s, bit):
            part = self.part(s)
            return copy(part, part, self.ss.at[s ^ bit], self.rs.at[s ^ bit], (d, flip(m, bit)))

        def take(self, s):
            if s and s not in self.got:
                self.got.add(s)
                part = self.part(s)
                copy(part, part, self.ss.at[s], self.rs.at[s], (d, flip(m, 1))).wait_recv()

        def begin(self):
            for s, bit in self.steps:
                if s == 0:
                    self.hop(s, bit).start()

        def rest(self):
            for s, bit in self.steps:
                if s:
                    self.take(s)
                    self.hop(s, bit).start()

        def all(self):
            for s in range(1, nmp):
                self.take(s)

        def finish(self):
            for s, bit in self.steps:
                self.hop(s, bit).wait_send()

    local = Gather(lambda s: weights.at[0:WIN + 1, across(s)], k_ss.at[0], k_rs.at[0])
    local_rows = Gather(lambda s: weights.at[WIN + 1, across(s)], k_ss.at[1], k_rs.at[1])
    foreign = {k: Gather(lambda s, k=k: rw_in.at[k - 1, across(s)], g_ss.at[k - 1], g_rs.at[k - 1])
               for k in range(1, WIN + 1)}
    stages = []
    for bits, peer in ((mp_bits, lambda o: (d, flip_all(m, o))), (dp_bits, lambda o: (flip_all(d, o), m))):
        for i in range(0, len(bits), 2):
            pair = bits[i:i + 2]
            stages.append([peer(sum(pair[:1]))] if len(pair) == 1 else [peer(o) for o in (*pair, sum(pair))])

    def loss_copies(i):
        return [copy(lsum.at[i], lin.at[i, j], l_ss.at[i, j], l_rs.at[i, j], dev) for j, dev in enumerate(stages[i])]

    def loss_step(i):
        if i:
            for j, c in enumerate(loss_copies(i - 1)):
                c.wait_recv()
            lsum[i] = functools.reduce(lambda x, y: x + y, [lin[i - 1, j] for j in range(len(stages[i - 1]))], lsum[i - 1])
        if i < len(stages):
            for c in loss_copies(i):
                c.start()

    qs.begin_direct(False, range(AHEAD, CHUNKS))
    local.begin()
    local_rows.begin()
    loss_step(0)

    def back(w, x):
        return lax.dot_general(w, x, COLS_BY_ROWS, preferred_element_type=jnp.float32)

    far = 1 - parity
    mid = (1 + far, half_of(1 - far))
    late = (2 - far, half_of(far))

    def grad_query(r):
        at = rows_of(r)
        out = jnp.dot(weights[0, at, :], p_ref[...], preferred_element_type=jnp.float32)
        for k in range(WIN):
            out = out + jnp.dot(weights[k + 1, at, :], pbuf[k], preferred_element_type=jnp.float32)
        gq_ref[at, :] = out.astype(jnp.bfloat16)

    def grad_passage(terms, start, end):
        for r in range(2):
            at = pl.ds(r * half, half)
            out = [back(w[:, at], x) for w, x in terms()]
            out = functools.reduce(lambda x, y: x + y, out)
            if not start:
                out = acc[at, :] + out
            if end:
                gp_ref[at, :] = out.astype(jnp.bfloat16)
            else:
                acc[at, :] = out

    def piece(slot, at):
        return rw_in.at[slot, at], qbuf[slot, at, :]

    def foreign_begin(k):
        dispatch(k).wait_recv()
        foreign[k].begin()

    for c in range(2, CHUNKS):
        qs.relay(c)
        if c == middle:
            loss_step(1)
        if c == CHUNKS - 2:
            foreign_begin(2)
    for k in (1, 3):
        foreign_begin(k)
    local.rest()
    if FIRST_Q <= first:
        qs.relay_late(first)
    local.all()
    local_rows.rest()
    for r in range(nmp):
        grad_query(r)
        if r == 1:
            if FIRST_Q <= first + 1:
                qs.relay_late(first + 1)
    for c in range(max(FIRST_Q, first + 2), CHUNKS):
        qs.relay_late(c)
    local_rows.all()
    grad_passage(lambda: [(weights.at[WIN + 1], q_ref[...])], True, False)
    for i in range(2, len(stages)):
        loss_step(i)
    for k in (2, 1, 3):
        foreign[k].rest()
    for k in (2, 1, 3):
        foreign[k].all()
    qs.early()
    grad_passage(lambda: [piece(0, half_of(0)), piece(0, half_of(1)), piece(1, half_of(0)), piece(*mid)], False, False)
    qs.late()
    grad_passage(lambda: [piece(*late)], False, False)
    loss_step(len(stages))
    total_count = functools.reduce(lambda x, y: x + y, [counts_ref[i] for i in range(ndp)])
    loss_ref[...] = lsum[len(stages), 0:1, 0:1] / total_count.astype(jnp.float32)
    qs.last()
    grad_passage(lambda: [piece(2, half_of(1))], False, True)

    ps.finish()
    qs.finish()
    for k in range(1, WIN + 1):
        dispatch(k).wait_send()
    for k in range(WIN + 1):
        for h in range(2):
            for j in range(1, nmp):
                tile_copy(k, h, j).wait_send()
    local.finish()
    local_rows.finish()
    for k in range(1, WIN + 1):
        foreign[k].finish()
    for i in range(len(stages)):
        for c in loss_copies(i):
            c.wait_send()


def local(ndp, nmp, query, passage, query_scale, passage_scale, partners, counts):
    rows, width = query.shape
    inv = 1.0 / math.sqrt(width * nmp)
    share = rows // nmp
    nst = sum(n.bit_length() // 2 for n in (ndp, nmp))
    bf, f32 = jnp.bfloat16, jnp.float32
    dma = pltpu.SemaphoreType.DMA
    vm = pl.BlockSpec(memory_space=pltpu.VMEM)
    hbm = pl.BlockSpec(memory_space=pltpu.HBM)
    gq, gp, loss = pl.pallas_call(
        functools.partial(kernel, ndp, nmp, inv),
        out_shape=[
            jax.ShapeDtypeStruct((rows, width), bf),
            jax.ShapeDtypeStruct((rows, width), bf),
            jax.ShapeDtypeStruct((1, 1), f32),
        ],
        in_specs=[hbm] * 6,
        out_specs=[vm] * 3,
        scratch_shapes=[
            pltpu.VMEM((rows, width), bf),
            pltpu.VMEM((rows, width), bf),
            pltpu.VMEM((rows,), bf),
            pltpu.VMEM((rows,), bf),
            pltpu.SMEM(partners.shape, jnp.int32),
            pltpu.SMEM(counts.shape, jnp.int32),
            pltpu.VMEM((WIN, rows, width), bf),
            pltpu.VMEM((WIN, rows, width), bf),
            pltpu.VMEM((8, rows), f32),
            pltpu.VMEM((WIN, 8, rows), f32),
            pltpu.VMEM((WIN + 1, 2, rows, rows // 2), f32),
            pltpu.VMEM((nmp - 1, WIN + 1, 2, share, rows // 2), f32),
            pltpu.VMEM((WIN + 2, rows, rows), bf),
            pltpu.VMEM((WIN, share, rows), bf),
            pltpu.VMEM((WIN, rows, rows), bf),
            pltpu.VMEM((rows, width), f32),
            pltpu.VMEM((nst + 1, 8, 128), f32),
            pltpu.VMEM((nst, 3, 8, 128), f32),
            dma((6,)),
            dma((4, CHUNKS + 1)), dma((WIN, CHUNKS + 1)),
            dma((4, CHUNKS + 1)), dma((WIN, CHUNKS + 1)),
            dma((nmp - 1, WIN + 1, 2)), dma((nmp - 1, WIN + 1, 2)),
            dma((2, nmp)), dma((2, nmp)),
            dma((WIN,)), dma((WIN,)),
            dma((WIN, nmp)), dma((WIN, nmp)),
            dma((nst, 3)), dma((nst, 3)),
        ],
        compiler_params=pltpu.CompilerParams(
            collective_id=0, has_side_effects=True, vmem_limit_bytes=48 * 1024 * 1024),
    )(*[pltpu.with_memory_space_constraint(x, pltpu.HBM)
        for x in (query, passage, passage_scale, query_scale, partners, counts)])
    return loss.reshape(()), gq, gp


def solution(mesh):
    return jax.shard_map(
        functools.partial(local, mesh.shape["dp"], mesh.shape["mp"]),
        mesh=mesh,
        in_specs=(P("dp", "mp"), P("dp", "mp"), P("dp"), P("dp"), P("dp", None), P()),
        out_specs=(P(), P("dp", "mp"), P("dp", "mp")),
        check_vma=False,
    )
```
